512 devices in a mesh: neuron: 128 (over z, y, core), trial: 4 (over x).
Axes of the slice: x: 4, y: 4, z: 16, core: 2. Of those that a mesh axis runs over, the one named last changes fastest.
Arguments:
- tensor: bfloat16 [8, 16384, 1024], P('trial', 'neuron'), may hold values from -1000 to 1000
- time_init: float32 [32, 1024], replicated, may hold values from -6 to 6
- trial_init: float32 [32, 8], P(None, 'trial'), may hold values from -6 to 6
Outputs:
- neuron_factor: float32 [32, 16384], P(None, 'neuron')
- time_factor: float32 [32, 1024], P(None, ('neuron', 'trial'))
- trial_factor: float32 [32, 8], P(None, 'trial')
The draws below stay inside these ranges and needn't reach their ends.
All inputs are finite; a program needn't handle non-finite values.
Results may differ from the reference program's by a relative error of at most 0.011.
Values may be sent and summed in bfloat16 or wider, within the bound.
No kernel may reach another device: no remote copies, remote signals or barrier semaphores. Data moves between devices by JAX's collectives and lax.ppermute only.
A program may use at most 64 MiB of HBM per device.

```python
import math
import jax
import jax.numpy as jnp
from jax import lax

TIMEPOINTS = 1024
COMPONENTS = 32
SWEEPS = 2
NEURONS = 16384
TRIALS = 8


def draw_tensor(key, part):
    key_list = jax.random.split(jax.random.fold_in(key, 11), 6)
    neuron_part = jax.random.truncated_normal(key_list[0], -4.0, 4.0, (COMPONENTS, NEURONS), jnp.float32)
    time_part = jax.random.truncated_normal(key_list[1], -4.0, 4.0, (COMPONENTS, TIMEPOINTS), jnp.float32)
    trial_part = jax.random.truncated_normal(key_list[2], -4.0, 4.0, (COMPONENTS, TRIALS), jnp.float32)
    strength = jnp.exp(jax.random.uniform(key_list[3], (COMPONENTS,), jnp.float32, math.log(0.3), math.log(3.0)))
    places = jnp.arange(NEURONS, dtype=jnp.float32) / NEURONS
    spread = jnp.exp(jax.random.uniform(key_list[4], (NEURONS,), jnp.float32, 0.0, math.log(10.0)))
    ramp_up = jnp.exp(0.5 * math.log(3.0) * places)
    row_scale = spread * ramp_up / 4.0

    def one_trial(trial_index):
        noise_key = jax.random.fold_in(key_list[5], trial_index)
        noise_part = jax.random.truncated_normal(noise_key, -4.0, 4.0, (NEURONS, TIMEPOINTS), jnp.float32)
        mixing = trial_part[:, trial_index] * strength / math.sqrt(COMPONENTS)
        signal = lax.dot_general(neuron_part * mixing[:, None], time_part, (((0,), (0,)), ((), ())), precision=lax.Precision.HIGHEST, preferred_element_type=jnp.float32)
        return (row_scale[:, None] * (signal + 0.7 * noise_part)).astype(jnp.bfloat16)
    return lax.map(one_trial, jnp.arange(TRIALS, dtype=jnp.int32))


def level_of(own_key, shape, cuts, least, top_value):
    def one(dim, blocks):
        steps = jax.random.uniform(jax.random.fold_in(jax.random.fold_in(own_key, 6), dim), (blocks,), jnp.float32, least / len(cuts), top_value / len(cuts))
        return jnp.repeat(jnp.exp(steps), shape[dim] // blocks).reshape((-1,) + (1,) * (len(shape) - dim - 1))

    loudness = one(*cuts[0])
    for cut in cuts[1:]:
        loudness = loudness * one(*cut)
    return loudness


def normal_values(rng, dims, deviation, reach, cuts=(), kind=jnp.bfloat16):
    factor_of = level_of(rng, dims, cuts, -0.22, 0.18) if cuts else 1.0
    values = jax.random.normal(rng, dims, jnp.float32) * deviation * factor_of
    return jnp.minimum(jnp.maximum(values, -reach), reach).astype(kind)


def setup_inputs(seed: int = 0) -> dict:
    keys = jax.random.split(jax.random.key(seed), 4)
    return {
        "tensor": draw_tensor(jax.random.fold_in(keys[3], 71), 0),
        "time_init": normal_values(keys[1], (COMPONENTS, TIMEPOINTS), 1.0, 6.0, (), jnp.float32),
        "trial_init": normal_values(keys[2], (COMPONENTS, TRIALS), 1.0, 6.0, ((1, 4),), jnp.float32),
    }


ridge_share = 0.1
tiny_eps = 1e-06

def gram_of(matrix):
    return lax.dot_general(matrix.astype(jnp.float32), matrix.astype(jnp.float32), (((1,), (1,)), ((), ())), precision=lax.Precision.HIGHEST, preferred_element_type=jnp.float32)

def damped_solve(gram_mat, right_hand):
    order_size = gram_mat.shape[0]
    identity_mat = jnp.eye(order_size, dtype=jnp.float32)
    damped = gram_mat + ridge_share * (jnp.trace(gram_mat) / order_size) * identity_mat
    cholesky_low = jnp.linalg.cholesky(damped)
    return jax.scipy.linalg.cho_solve((cholesky_low, True), right_hand)

def reference(tensor, time_init, trial_init):
    time_now = time_init
    trial_now = trial_init
    neuron_now = jnp.zeros((time_init.shape[0], tensor.shape[1]), jnp.float32)
    for sweep_index in range(SWEEPS):
        time_rounded = time_now.astype(jnp.bfloat16)

        def project_one(trial_slab):
            return lax.dot_general(time_rounded.astype(jnp.float32), trial_slab.astype(jnp.float32), (((1,), (1,)), ((), ())), preferred_element_type=jnp.float32)
        projected = lax.map(project_one, tensor)
        time_gram = gram_of(time_now)
        trial_gram = gram_of(trial_now)
        neuron_terms = lax.optimization_barrier(jnp.sum(trial_now.T[:, :, None] * projected, axis=0))
        neuron_raw = damped_solve(trial_gram * time_gram, neuron_terms)
        neuron_now = neuron_raw / jnp.sqrt(lax.optimization_barrier(jnp.mean(neuron_raw * neuron_raw, axis=1, keepdims=True)) + tiny_eps)
        neuron_gram = gram_of(neuron_now)
        trial_terms = lax.optimization_barrier(jnp.sum(neuron_now[None] * projected, axis=2)).T
        trial_now = damped_solve(neuron_gram * time_gram, trial_terms)
        trial_gram = gram_of(trial_now)
        weights = (neuron_now[None] * trial_now.T[:, :, None]).astype(jnp.bfloat16)

        def accumulate(running, paired):
            return (running + jnp.dot(paired[0].astype(jnp.float32), paired[1].astype(jnp.float32), preferred_element_type=jnp.float32), None)
        time_terms, unused = lax.scan(accumulate, jnp.zeros(time_now.shape, jnp.float32), (weights, tensor))
        time_raw = damped_solve(neuron_gram * trial_gram, time_terms)
        time_now = time_raw / jnp.sqrt(lax.optimization_barrier(jnp.mean(time_raw * time_raw, axis=1, keepdims=True)) + tiny_eps)
    return (neuron_now, time_now, trial_now)
```

```python
import jax
import jax.numpy as jnp
from jax import lax
from jax.sharding import PartitionSpec as P

SWEEPS = 2


ridge_share = 0.1
tiny_eps = 1e-06
EXACT = lax.Precision.HIGHEST


def gram_of(matrix):
    return lax.dot_general(
        matrix,
        matrix,
        (((1,), (1,)), ((), ())),
        precision=EXACT,
        preferred_element_type=jnp.float32,
    )


def damped_solve(gram_mat, right_hand):
    order_size = gram_mat.shape[0]
    identity_mat = jnp.eye(order_size, dtype=jnp.float32)
    damped = gram_mat + ridge_share * (jnp.trace(gram_mat) / order_size) * identity_mat
    cholesky_low = jnp.linalg.cholesky(damped)
    return jax.scipy.linalg.cho_solve((cholesky_low, True), right_hand)


def to_rows(*pieces):
    flat = jnp.concatenate([piece.reshape(-1) for piece in pieces])
    spare = -flat.shape[0] % 128
    return jnp.pad(flat, (0, spare)).reshape(-1, 128)


def from_rows(rows, *shapes):
    flat = rows.reshape(rows.shape[0], -1)
    taken, start = [], 0
    for shape in shapes:
        size = 1
        for extent in shape:
            size *= extent
        taken.append(flat[:, start : start + size].reshape((rows.shape[0],) + shape))
        start += size
    return taken


def share_all(rows, axis):
    members = lax.axis_size(axis)
    return lax.all_to_all(jnp.broadcast_to(rows[None], (members,) + rows.shape), axis, 0, 0)


def per_device(tensor, time_init, trial_init):
    own_trials, own_neurons, timepoints = tensor.shape
    components = time_init.shape[0]
    blocks, planes = lax.axis_size("neuron"), lax.axis_size("trial")
    neuron_count = own_neurons * blocks
    trial_count = own_trials * planes
    width = timepoints // blocks
    plane = lax.axis_index("trial")
    gram_rows = components // planes

    time_now = time_init
    trial_now = None
    for sweep_index in range(SWEEPS):
        time_gram = gram_of(time_now)
        projected = jnp.einsum(
            "rj,kij->kri",
            time_now.astype(jnp.bfloat16),
            tensor,
            preferred_element_type=jnp.float32,
        )
        if trial_now is None:
            own_trial = trial_init
        else:
            own_trial = lax.dynamic_slice_in_dim(trial_now, plane * own_trials, own_trials, 1)
        local_terms = jnp.sum(own_trial.T[:, :, None] * projected, axis=0)
        if trial_now is None:
            shared = share_all(
                jnp.concatenate([local_terms, to_rows(trial_init)], axis=0), "trial"
            )
            neuron_terms = jnp.sum(shared[:, :components], axis=0)
            (columns,) = from_rows(shared[:, components:], (components, own_trials))
            trial_now = columns.transpose(1, 0, 2).reshape(components, trial_count)
        else:
            neuron_terms = jnp.sum(share_all(local_terms, "trial"), axis=0)
        raw = damped_solve(gram_of(trial_now) * time_gram, neuron_terms)

        own_rows = lax.dynamic_slice_in_dim(raw, plane * gram_rows, gram_rows, 0)
        gram_part = lax.dot_general(
            own_rows, raw, (((1,), (1,)), ((), ())),
            precision=EXACT, preferred_element_type=jnp.float32,
        )
        terms_part = jnp.sum(raw[None] * projected, axis=2)
        partial = jnp.einsum(
            "ri,kij->krj", raw.astype(jnp.bfloat16), tensor, preferred_element_type=jnp.float32
        )
        chunks = partial.reshape(own_trials * components, width, blocks)
        chunks = chunks.transpose(2, 1, 0).reshape(blocks, -1, 128)
        small = to_rows(gram_part, terms_part)
        small_hi = small.astype(jnp.bfloat16)
        small_lo = (small - small_hi.astype(jnp.float32)).astype(jnp.bfloat16)
        small = jnp.concatenate([small_hi, small_lo], axis=0)
        sent = jnp.concatenate(
            [
                chunks.astype(jnp.bfloat16),
                jnp.broadcast_to(small[None], (blocks,) + small.shape),
            ],
            axis=1,
        )
        got = lax.all_to_all(sent, "neuron", 0, 0).astype(jnp.float32)
        summed = jnp.sum(got, axis=0)
        chunk_rows = chunks.shape[1]
        small_rows = small_hi.shape[0]
        merged = jnp.concatenate(
            [
                summed[:chunk_rows],
                summed[chunk_rows : chunk_rows + small_rows] + summed[chunk_rows + small_rows :],
            ],
            axis=0,
        )
        shared = share_all(merged, "trial")
        columns, gram_all, terms_all = from_rows(
            shared,
            (width, own_trials, components),
            (gram_rows, components),
            (own_trials, components),
        )
        raw_gram = gram_all.reshape(components, components)
        scaling = 1.0 / jnp.sqrt(jnp.diagonal(raw_gram) / neuron_count + tiny_eps)
        neuron_now = raw * scaling[:, None]
        neuron_gram = scaling[:, None] * raw_gram * scaling[None, :]
        trial_terms = terms_all.reshape(trial_count, components).T * scaling[:, None]
        trial_now = damped_solve(neuron_gram * time_gram, trial_terms)
        trial_gram = gram_of(trial_now)
        weighted = columns * trial_now.T.reshape(planes, 1, own_trials, components)
        time_terms = jnp.sum(weighted, axis=(0, 2)).T * scaling[:, None]
        time_part = damped_solve(neuron_gram * trial_gram, time_terms)
        gathered = share_all(to_rows(time_part.T), "neuron")
        (gathered,) = from_rows(gathered, (width, components))
        time_raw = gathered.transpose(2, 1, 0).reshape(components, timepoints)
        time_now = time_raw / jnp.sqrt(
            jnp.mean(time_raw * time_raw, axis=1, keepdims=True) + tiny_eps
        )
    position = lax.axis_index(("neuron", "trial"))
    share_width = timepoints // (blocks * planes)
    time_out = lax.dynamic_slice_in_dim(time_now, position * share_width, share_width, 1)
    trial_out = lax.dynamic_slice_in_dim(trial_now, plane * own_trials, own_trials, 1)
    return (neuron_now, time_out, trial_out)


def solution(mesh):
    placed = (P("trial", "neuron", None), P(), P(None, "trial"))
    return jax.shard_map(
        per_device,
        mesh=mesh,
        in_specs=placed,
        out_specs=(P(None, "neuron"), P(None, ("neuron", "trial")), P(None, "trial")),
        check_vma=False,
    )
```

```python
import jax
import jax.numpy as jnp
from jax import lax
from jax.experimental import pallas as pl
from jax.sharding import Mesh, PartitionSpec as P

SWEEPS = 2


ridge_share = 0.1
tiny_eps = 1e-06
EXACT = lax.Precision.HIGHEST
LANES = 128


def gram_of(matrix):
    return lax.dot_general(
        matrix,
        matrix,
        (((1,), (1,)), ((), ())),
        precision=EXACT,
        preferred_element_type=jnp.float32,
    )


def product(left, right):
    return lax.dot_general(
        left,
        right,
        (((1,), (0,)), ((), ())),
        precision=EXACT,
        preferred_element_type=jnp.float32,
    )


def damped_inverse(system):
    size = system.shape[0]
    rows = lax.broadcasted_iota(jnp.int32, (size, size), 0)
    cols = lax.broadcasted_iota(jnp.int32, (size, size), 1)
    eye = (rows == cols).astype(jnp.float32)
    trace = jnp.sum(jnp.sum(system * eye, axis=1, keepdims=True), axis=0, keepdims=True)
    damped = system + ridge_share * (trace / size) * eye
    both = jnp.concatenate([damped, eye], axis=1)
    row = lax.broadcasted_iota(jnp.int32, (size, 1), 0)
    for step in range(size):
        pivot_row = both[step : step + 1, :] / both[step : step + 1, step : step + 1]
        cleared = both - both[:, step : step + 1] * pivot_row
        both = jnp.where(row == step, pivot_row, cleared)
    return both[:, size:]


def inverse_body(left_ref, right_ref, out_ref):
    out_ref[...] = damped_inverse(left_ref[...] * right_ref[...])


def inverse_of(left, right):
    return pl.pallas_call(
        inverse_body, out_shape=jax.ShapeDtypeStruct(left.shape, jnp.float32)
    )(left, right)


def share_all(rows, axis):
    members = lax.axis_size(axis)
    return lax.all_to_all(jnp.broadcast_to(rows[None], (members,) + rows.shape), axis, 0, 0)


def per_device(tensor, time_init, trial_init):
    own_trials, own_neurons, timepoints = tensor.shape
    components = time_init.shape[0]
    planes = lax.axis_size("x")
    blocks = lax.axis_size(("y", "core"))
    neuron_count = own_neurons * blocks * lax.axis_size("z")
    trial_count = own_trials * planes
    width = timepoints // blocks
    plane = lax.axis_index("x")
    q_rows = own_trials * components

    time_now = time_init
    trial_now = None
    trial_gram = None
    for sweep_index in range(SWEEPS):
        time_gram = gram_of(time_now)
        projected = jnp.einsum(
            "rj,kij->kri",
            time_now.astype(jnp.bfloat16),
            tensor,
            preferred_element_type=jnp.float32,
        ).reshape(q_rows, own_neurons)
        if trial_now is None:
            padded = jnp.pad(trial_init, ((0, 0), (0, own_neurons - own_trials)))
            shared = share_all(jnp.concatenate([projected, padded], axis=0), "x")
            trial_now = jnp.concatenate(
                [shared[member, q_rows:, :own_trials] for member in range(planes)], axis=1
            )
            trial_gram = gram_of(trial_now)
            shared = shared[:, :q_rows]
        else:
            shared = share_all(projected, "x")
        projected = shared.reshape(trial_count, components, own_neurons)
        neuron_terms = jnp.sum(trial_now.T[:, :, None] * projected, axis=0)
        raw = product(inverse_of(trial_gram, time_gram), neuron_terms)

        raw_gram = gram_of(raw)
        terms = jnp.sum(raw[None] * projected, axis=2).T
        partial = jnp.einsum(
            "ri,kij->krj", raw.astype(jnp.bfloat16), tensor, preferred_element_type=jnp.float32
        ).reshape(q_rows, blocks, width)
        small = jnp.concatenate(
            [
                raw_gram,
                terms,
                jnp.zeros((components, width - components - trial_count), jnp.float32),
            ],
            axis=1,
        )
        sent = jnp.concatenate(
            [partial.transpose(1, 0, 2), jnp.broadcast_to(small[None], (blocks,) + small.shape)],
            axis=1,
        )
        summed = jnp.sum(lax.all_to_all(sent, ("y", "core"), 0, 0), axis=0)
        rounded = lax.reduce_precision(summed, 8, 7)
        rest = summed[q_rows:] - rounded[q_rows:]
        halves = jnp.concatenate([rounded, rest], axis=0).astype(jnp.bfloat16)
        got = share_all(halves, "z").astype(jnp.float32)
        summed = jnp.sum(got, axis=0)
        columns = summed[:q_rows].reshape(own_trials, components, width)
        small = summed[q_rows : q_rows + components] + summed[q_rows + components :]
        raw_gram = small[:, :components]
        terms = small[:, components : components + trial_count]
        scaling = 1.0 / jnp.sqrt(jnp.diagonal(raw_gram) / neuron_count + tiny_eps)
        neuron_now = raw * scaling[:, None]
        neuron_gram = scaling[:, None] * raw_gram * scaling[None, :]
        trial_now = product(inverse_of(neuron_gram, time_gram), terms * scaling[:, None])
        trial_gram = gram_of(trial_now)
        own_trial = lax.dynamic_slice_in_dim(trial_now, plane * own_trials, own_trials, 1)
        weighted = jnp.sum(own_trial.T[:, :, None] * columns, axis=0) * scaling[:, None]
        gathered = share_all(weighted, ("y", "core", "x"))
        time_inverse = inverse_of(neuron_gram, trial_gram)
        gathered = jnp.sum(gathered.reshape(blocks, planes, components, width), axis=1)
        time_terms = gathered.transpose(1, 0, 2).reshape(components, timepoints)
        time_raw = product(time_inverse, time_terms)
        time_now = time_raw / jnp.sqrt(
            jnp.mean(time_raw * time_raw, axis=1, keepdims=True) + tiny_eps
        )
    position = lax.axis_index(("z", "y", "core", "x"))
    share_width = timepoints // lax.axis_size(("z", "y", "core", "x"))
    time_out = lax.dynamic_slice_in_dim(time_now, position * share_width, share_width, 1)
    trial_out = lax.dynamic_slice_in_dim(trial_now, plane * own_trials, own_trials, 1)
    return (neuron_now, time_out, trial_out)


def solution(mesh):
    neuron, trial = mesh.shape["neuron"], mesh.shape["trial"]
    layers = max(neuron // 8, 1)
    fine = Mesh(
        mesh.devices.reshape(layers, neuron // layers // 2, 2, trial), ("z", "y", "core", "x")
    )
    rows = ("z", "y", "core")
    return jax.shard_map(
        per_device,
        mesh=fine,
        in_specs=(P("x", rows, None), P(), P(None, "x")),
        out_specs=(P(None, rows), P(None, rows + ("x",)), P(None, "x")),
        check_vma=False,
    )
```

```python
import jax
import jax.numpy as jnp
from jax import lax
from jax.experimental import pallas as pl
from jax.experimental.pallas import tpu as pltpu
from jax.sharding import Mesh, PartitionSpec as P

SWEEPS = 2


ridge_share = 0.1
tiny_eps = 1e-06
EXACT = lax.Precision.HIGHEST
PART = 8
WIRE = jnp.bfloat16


def gram_of(matrix):
    return lax.dot_general(
        matrix,
        matrix,
        (((1,), (1,)), ((), ())),
        precision=EXACT,
        preferred_element_type=jnp.float32,
    )


def product(left, right):
    return lax.dot_general(
        left,
        right,
        (((1,), (0,)), ((), ())),
        precision=EXACT,
        preferred_element_type=jnp.float32,
    )


def eye_of(size):
    rows = lax.broadcasted_iota(jnp.int32, (size, size), 0)
    cols = lax.broadcasted_iota(jnp.int32, (size, size), 1)
    return (rows == cols).astype(jnp.float32)


def damped_inverse(system):
    size = system.shape[0]
    eye = eye_of(size)
    trace = jnp.sum(jnp.sum(system * eye, axis=1, keepdims=True), axis=0, keepdims=True)
    share = size / trace
    both = jnp.concatenate([system * share + ridge_share * eye, eye], axis=1)
    row = lax.broadcasted_iota(jnp.int32, both.shape, 0)
    for step in range(0, size, 2):
        first = jnp.broadcast_to(both[:, step : step + 1], both.shape)
        second = jnp.broadcast_to(both[:, step + 1 : step + 2], both.shape)
        upper, lower = both[step : step + 1], both[step + 1 : step + 2]
        p00, p01 = first[step : step + 1], second[step : step + 1]
        p10, p11 = first[step + 1 : step + 2], second[step + 1 : step + 2]
        over = 1.0 / (p00 * p11 - p01 * p10)
        new_upper = (p11 * upper - p01 * lower) * over
        new_lower = (p00 * lower - p10 * upper) * over
        cleared = both - first * new_upper - second * new_lower
        both = jnp.where(row == step, new_upper, jnp.where(row == step + 1, new_lower, cleared))
    return both[:, size:] * share


def pack_small(gram, terms):
    size = gram.shape[0]
    pieces = []
    for start in range(0, size, PART):
        pieces.append(gram[start : start + PART, start:])
    for start in range(0, size, PART):
        pieces.append(terms[start : start + PART])
    used = sum(piece.shape[1] for piece in pieces)
    pieces.append(jnp.zeros((PART, 128 - used), jnp.float32))
    return jnp.concatenate(pieces, axis=1)


def unpack_small(tile, size, count):
    rows, place = [], 0
    for start in range(0, size, PART):
        piece = tile[:, place : place + size - start]
        place += size - start
        if start:
            piece = jnp.concatenate([jnp.zeros((PART, start), jnp.float32), piece], axis=1)
        rows.append(piece)
    upper = jnp.concatenate(rows, axis=0)
    terms = []
    for start in range(0, size, PART):
        terms.append(tile[:, place : place + count])
        place += count
    row_part = lax.broadcasted_iota(jnp.int32, (size, size), 0) // PART
    col_part = lax.broadcasted_iota(jnp.int32, (size, size), 1) // PART
    return jnp.where(col_part >= row_part, upper, upper.T), jnp.concatenate(terms, axis=0)


def call(body, outs, *args, smem=()):
    specs = [
        pl.BlockSpec(memory_space=pltpu.SMEM if place in smem else pltpu.VMEM)
        for place in range(len(args))
    ]
    return pl.pallas_call(
        body,
        out_shape=outs,
        in_specs=specs,
        out_specs=jax.tree.map(lambda out: pl.BlockSpec(memory_space=pltpu.VMEM), outs),
    )(*args)


def put_projected(time_now, tensor_ref, sent_ref):
    rounded = time_now.astype(jnp.bfloat16)
    size = time_now.shape[0]
    for trial in range(tensor_ref.shape[0]):
        projected = lax.dot_general(
            rounded,
            tensor_ref[trial],
            (((1,), (1,)), ((), ())),
            preferred_element_type=jnp.float32,
        )
        for member in range(sent_ref.shape[0]):
            sent_ref[member, trial * size : (trial + 1) * size, :] = projected


def project_body(time_ref, trial_ref, tensor_ref, sent_ref):
    put_projected(time_ref[...], tensor_ref, sent_ref)
    size, count = trial_ref.shape
    lanes = sent_ref.shape[2]
    tile = jnp.concatenate([trial_ref[...], jnp.zeros((size, lanes - count), jnp.float32)], axis=1)
    for member in range(sent_ref.shape[0]):
        sent_ref[member, tensor_ref.shape[0] * size :, :] = tile


def put_neuron(trial_now, inverse, shared_ref, tensor_ref, raw_ref, sent_ref):
    size, trial_count = trial_now.shape
    own_trials = tensor_ref.shape[0]
    terms = []
    projected = []
    for trial in range(trial_count):
        start = trial % own_trials * size
        projected.append(shared_ref[trial // own_trials, start : start + size, :])
    neuron_terms = trial_now[:, 0:1] * projected[0]
    for trial in range(1, trial_count):
        neuron_terms = neuron_terms + trial_now[:, trial : trial + 1] * projected[trial]
    raw = product(inverse, neuron_terms)
    raw_ref[...] = raw
    lane = lax.broadcasted_iota(jnp.int32, (size, trial_count), 1)
    terms = jnp.zeros((size, trial_count), jnp.float32)
    for trial in range(trial_count):
        one = jnp.sum(raw * projected[trial], axis=1, keepdims=True)
        terms = jnp.where(lane == trial, one, terms)
    small = pack_small(gram_of(raw), terms)
    blocks, rows, width = sent_ref.shape
    rounded = raw.astype(jnp.bfloat16)
    for trial in range(own_trials):
        partial = jnp.dot(rounded, tensor_ref[trial], preferred_element_type=jnp.float32)
        for block in range(blocks):
            sent_ref[block, trial * size : (trial + 1) * size, :] = partial[
                :, block * width : (block + 1) * width
            ]
    for block in range(blocks):
        sent_ref[block, own_trials * size :, :] = small


def first_neuron_body(shared_ref, gram_ref, tensor_ref, raw_ref, sent_ref):
    own_trials = tensor_ref.shape[0]
    size = raw_ref.shape[0]
    columns = [
        shared_ref[member, own_trials * size :, :own_trials]
        for member in range(shared_ref.shape[0])
    ]
    trial_now = jnp.concatenate(columns, axis=1)
    inverse = damped_inverse(gram_of(trial_now) * gram_ref[...])
    put_neuron(trial_now, inverse, shared_ref, tensor_ref, raw_ref, sent_ref)


def neuron_body(shared_ref, trial_ref, inverse_ref, tensor_ref, raw_ref, sent_ref):
    put_neuron(trial_ref[...], inverse_ref[...], shared_ref, tensor_ref, raw_ref, sent_ref)


def reduce_body(got_ref, sent_ref):
    total = got_ref[0]
    for member in range(1, got_ref.shape[0]):
        total = total + got_ref[member]
    rounded = total.astype(WIRE)
    main = total.shape[0] - PART
    small = total[main:]
    high = small.astype(WIRE).astype(jnp.float32)
    halves = jnp.concatenate([high, small - high], axis=0).astype(WIRE)
    for member in range(sent_ref.shape[0]):
        sent_ref[member, :main, :] = rounded[:main]
        sent_ref[member, main:, :] = halves


def finish_body(neuron_count, plane_ref, got_ref, gram_ref, raw_ref, *outs):
    neuron_ref, neuron_gram_ref, trial_ref, trial_gram_ref, own_ref, sent_ref = outs
    size = raw_ref.shape[0]
    trial_count = trial_ref.shape[1]
    own_trials = own_ref.shape[1]
    total = got_ref[0].astype(jnp.float32)
    for member in range(1, got_ref.shape[0]):
        total = total + got_ref[member].astype(jnp.float32)
    main = own_trials * size
    small = total[main : main + PART] + total[main + PART :]
    raw_gram, terms = unpack_small(small, size, trial_count)
    diagonal = raw_gram * eye_of(size)
    down = 1.0 / jnp.sqrt(jnp.sum(diagonal, axis=1, keepdims=True) / neuron_count + tiny_eps)
    across = 1.0 / jnp.sqrt(jnp.sum(diagonal, axis=0, keepdims=True) / neuron_count + tiny_eps)
    neuron_ref[...] = raw_ref[...] * down
    neuron_gram = down * raw_gram * across
    neuron_gram_ref[...] = neuron_gram
    trial_now = product(damped_inverse(neuron_gram * gram_ref[...]), terms * down)
    trial_ref[...] = trial_now
    trial_gram_ref[...] = gram_of(trial_now)
    lane = lax.broadcasted_iota(jnp.int32, trial_now.shape, 1)
    weighted = None
    for trial in range(own_trials):
        mine = lane == plane_ref[0] * own_trials + trial
        column = jnp.sum(jnp.where(mine, trial_now, 0.0), axis=1, keepdims=True)
        own_ref[:, trial : trial + 1] = column
        part = column * total[trial * size : (trial + 1) * size]
        weighted = part if weighted is None else weighted + part
    weighted = weighted * down
    for member in range(sent_ref.shape[0]):
        sent_ref[member] = weighted


def inverse_body(left_ref, right_ref, out_ref):
    out_ref[...] = damped_inverse(left_ref[...] * right_ref[...])


def time_of(planes, got_ref, inverse_ref):
    pieces = []
    for block in range(got_ref.shape[0] // planes):
        piece = got_ref[block * planes]
        for plane in range(1, planes):
            piece = piece + got_ref[block * planes + plane]
        pieces.append(piece)
    raw = product(inverse_ref[...], jnp.concatenate(pieces, axis=1))
    mean = jnp.sum(raw * raw, axis=1, keepdims=True) / raw.shape[1]
    return raw / jnp.sqrt(mean + tiny_eps)


def next_body(planes, got_ref, inverse_ref, tensor_ref, time_ref, sent_ref):
    time_now = time_of(planes, got_ref, inverse_ref)
    time_ref[...] = time_now
    put_projected(time_now, tensor_ref, sent_ref)


def gram_body(time_ref, gram_ref):
    gram_ref[...] = gram_of(time_ref[...])


def next_inverse_body(time_ref, trial_gram_ref, gram_ref, inverse_ref):
    gram = gram_of(time_ref[...])
    gram_ref[...] = gram
    inverse_ref[...] = damped_inverse(gram * trial_gram_ref[...])


def last_body(planes, got_ref, inverse_ref, time_ref):
    time_ref[...] = time_of(planes, got_ref, inverse_ref)


def per_device(tensor, time_init, trial_init):
    own_trials, own_neurons, timepoints = tensor.shape
    components = time_init.shape[0]
    planes = lax.axis_size("x")
    short = ("y", "core")
    blocks = lax.axis_size(short)
    layers = lax.axis_size("z")
    neuron_count = own_neurons * blocks * layers
    trial_count = own_trials * planes
    width = timepoints // blocks
    main = own_trials * components
    plane = lax.axis_index("x").astype(jnp.int32).reshape(1)

    def shape(*dims, kind=jnp.float32):
        return jax.ShapeDtypeStruct(dims, kind)

    square = shape(components, components)
    neuron_outs = (shape(components, own_neurons), shape(blocks, main + PART, width))
    shared = call(
        project_body,
        shape(planes, main + components, own_neurons),
        time_init,
        trial_init,
        tensor,
    )
    shared = lax.all_to_all(shared, "x", 0, 0)
    time_gram = call(gram_body, square, time_init)
    raw, sent = call(first_neuron_body, neuron_outs, shared, time_gram, tensor)
    for sweep_index in range(SWEEPS):
        got = lax.all_to_all(sent, short, 0, 0)
        sent = call(reduce_body, shape(layers, main + 2 * PART, width, kind=WIRE), got)
        got = lax.all_to_all(sent, "z", 0, 0)
        neuron_now, neuron_gram, trial_now, trial_gram, own_trial, sent = call(
            lambda *refs: finish_body(neuron_count, *refs),
            (
                shape(components, own_neurons),
                square,
                shape(components, trial_count),
                square,
                shape(components, own_trials),
                shape(blocks * planes, components, width),
            ),
            plane,
            got,
            time_gram,
            raw,
            smem=(0,),
        )
        got = lax.all_to_all(sent, short + ("x",), 0, 0)
        inverse = call(inverse_body, square, neuron_gram, trial_gram)
        if sweep_index == SWEEPS - 1:
            time_now = call(
                lambda *refs: last_body(planes, *refs),
                shape(components, timepoints),
                got,
                inverse,
            )
            break
        time_now, shared = call(
            lambda *refs: next_body(planes, *refs),
            (shape(components, timepoints), shape(planes, main, own_neurons)),
            got,
            inverse,
            tensor,
        )
        shared = lax.all_to_all(shared, "x", 0, 0)
        time_gram, inverse = call(next_inverse_body, (square, square), time_now, trial_gram)
        raw, sent = call(neuron_body, neuron_outs, shared, trial_now, inverse, tensor)
    position = lax.axis_index(("z", "y", "core", "x"))
    share_width = timepoints // (layers * blocks * planes)
    time_out = lax.dynamic_slice_in_dim(time_now, position * share_width, share_width, 1)
    return (neuron_now, time_out, own_trial)


def solution(mesh):
    neuron, trial = mesh.shape["neuron"], mesh.shape["trial"]
    layers = max(neuron // 8, 1)
    fine = Mesh(
        mesh.devices.reshape(layers, neuron // layers // 2, 2, trial), ("z", "y", "core", "x")
    )
    rows = ("z", "y", "core")
    return jax.shard_map(
        per_device,
        mesh=fine,
        in_specs=(P("x", rows, None), P(), P(None, "x")),
        out_specs=(P(None, rows), P(None, rows + ("x",)), P(None, "x")),
        check_vma=False,
    )
```

```python
import jax
import jax.numpy as jnp
from jax import lax
from jax.experimental import pallas as pl
from jax.experimental.pallas import tpu as pltpu
from jax.sharding import Mesh, PartitionSpec as P

SWEEPS = 2


ridge_share = 0.1
tiny_eps = 1e-06
EXACT = lax.Precision.HIGHEST
PART = 8
WIRE = jnp.bfloat16


def gram_of(matrix):
    return lax.dot_general(
        matrix,
        matrix,
        (((1,), (1,)), ((), ())),
        precision=EXACT,
        preferred_element_type=jnp.float32,
    )


def product(left, right):
    return lax.dot_general(
        left,
        right,
        (((1,), (0,)), ((), ())),
        precision=EXACT,
        preferred_element_type=jnp.float32,
    )


def rows_product(left, right):
    return lax.dot_general(
        left,
        right,
        (((1,), (1,)), ((), ())),
        precision=EXACT,
        preferred_element_type=jnp.float32,
    )


def split(values):
    high = values.astype(WIRE).astype(jnp.float32)
    return jnp.concatenate([high, values - high], axis=0).astype(WIRE)


def eye_of(size):
    rows = lax.broadcasted_iota(jnp.int32, (size, size), 0)
    cols = lax.broadcasted_iota(jnp.int32, (size, size), 1)
    return (rows == cols).astype(jnp.float32)


def damped_inverse(system):
    size = system.shape[0]
    eye = eye_of(size)
    trace = jnp.sum(jnp.sum(system * eye, axis=1, keepdims=True), axis=0, keepdims=True)
    share = size / trace
    both = jnp.concatenate([system * share + ridge_share * eye, eye], axis=1)
    row = lax.broadcasted_iota(jnp.int32, both.shape, 0)
    for step in range(0, size, 2):
        first = jnp.broadcast_to(both[:, step : step + 1], both.shape)
        second = jnp.broadcast_to(both[:, step + 1 : step + 2], both.shape)
        upper, lower = both[step : step + 1], both[step + 1 : step + 2]
        p00, p01 = first[step : step + 1], second[step : step + 1]
        p10, p11 = first[step + 1 : step + 2], second[step + 1 : step + 2]
        over = 1.0 / (p00 * p11 - p01 * p10)
        new_upper = (p11 * upper - p01 * lower) * over
        new_lower = (p00 * lower - p10 * upper) * over
        cleared = both - first * new_upper - second * new_lower
        both = jnp.where(row == step, new_upper, jnp.where(row == step + 1, new_lower, cleared))
    return both[:, size:] * share


def pack_small(gram, terms):
    size = gram.shape[0]
    pieces = []
    for start in range(0, size, PART):
        pieces.append(gram[start : start + PART, start:])
    for start in range(0, size, PART):
        pieces.append(terms[start : start + PART])
    used = sum(piece.shape[1] for piece in pieces)
    pieces.append(jnp.zeros((PART, 128 - used), jnp.float32))
    return jnp.concatenate(pieces, axis=1)


def unpack_small(tile, size, count):
    rows, place = [], 0
    for start in range(0, size, PART):
        piece = tile[:, place : place + size - start]
        place += size - start
        if start:
            piece = jnp.concatenate([jnp.zeros((PART, start), jnp.float32), piece], axis=1)
        rows.append(piece)
    upper = jnp.concatenate(rows, axis=0)
    terms = []
    for start in range(0, size, PART):
        terms.append(tile[:, place : place + count])
        place += count
    row_part = lax.broadcasted_iota(jnp.int32, (size, size), 0) // PART
    col_part = lax.broadcasted_iota(jnp.int32, (size, size), 1) // PART
    return jnp.where(col_part >= row_part, upper, upper.T), jnp.concatenate(terms, axis=0)


def call(body, outs, *args, smem=(), slow=()):
    single = not isinstance(outs, tuple)
    listed = (outs,) if single else outs
    specs = [
        pl.BlockSpec(memory_space=pltpu.SMEM if place in smem else pltpu.VMEM)
        for place in range(len(args))
    ]
    args = [
        arg if place in smem else pltpu.with_memory_space_constraint(arg, pltpu.VMEM)
        for place, arg in enumerate(args)
    ]
    shapes = tuple(
        out if place in slow else pltpu.VMEM(out.shape, out.dtype)
        for place, out in enumerate(listed)
    )
    result = pl.pallas_call(
        body,
        out_shape=shapes,
        in_specs=specs,
        out_specs=tuple(pl.BlockSpec(memory_space=pltpu.VMEM) for _ in listed),
    )(*args)
    return result[0] if single else result


def put_projected(time_now, tensor_ref, sent_ref):
    rounded = time_now.astype(jnp.bfloat16)
    size = time_now.shape[0]
    for trial in range(tensor_ref.shape[0]):
        projected = lax.dot_general(
            rounded,
            tensor_ref[trial],
            (((1,), (1,)), ((), ())),
            preferred_element_type=jnp.float32,
        )
        for member in range(sent_ref.shape[0]):
            sent_ref[member, trial * size : (trial + 1) * size, :] = projected


def project_body(time_ref, trial_ref, tensor_ref, sent_ref):
    put_projected(time_ref[...], tensor_ref, sent_ref)
    count, size = trial_ref.shape
    lanes = sent_ref.shape[2]
    tile = jnp.concatenate([trial_ref[...], jnp.zeros((PART - count, size), jnp.float32)], axis=0)
    tile = jnp.concatenate([tile, jnp.zeros((PART, lanes - size), jnp.float32)], axis=1)
    for member in range(sent_ref.shape[0]):
        sent_ref[member, count * size :, :] = tile


def put_neuron(trial_now, inverse, shared_ref, tensor_ref, raw_ref, sent_ref):
    size, trial_count = trial_now.shape
    own_trials = tensor_ref.shape[0]
    terms = []
    projected = []
    for trial in range(trial_count):
        start = trial % own_trials * size
        projected.append(shared_ref[trial // own_trials, start : start + size, :])
    neuron_terms = trial_now[:, 0:1] * projected[0]
    for trial in range(1, trial_count):
        neuron_terms = neuron_terms + trial_now[:, trial : trial + 1] * projected[trial]
    raw = product(inverse, neuron_terms)
    raw_ref[...] = raw
    lane = lax.broadcasted_iota(jnp.int32, (size, trial_count), 1)
    terms = jnp.zeros((size, trial_count), jnp.float32)
    for trial in range(trial_count):
        one = jnp.sum(raw * projected[trial], axis=1, keepdims=True)
        terms = jnp.where(lane == trial, one, terms)
    small = split(pack_small(gram_of(raw), terms))
    blocks, rows, width = sent_ref.shape
    rounded = raw.astype(jnp.bfloat16)
    for trial in range(own_trials):
        partial = jnp.dot(rounded, tensor_ref[trial], preferred_element_type=jnp.float32)
        partial = partial.astype(WIRE)
        for block in range(blocks):
            sent_ref[block, trial * size : (trial + 1) * size, :] = partial[
                :, block * width : (block + 1) * width
            ]
    for block in range(blocks):
        sent_ref[block, own_trials * size :, :] = small


def first_neuron_body(shared_ref, gram_ref, tensor_ref, raw_ref, sent_ref):
    own_trials = tensor_ref.shape[0]
    size = raw_ref.shape[0]
    main = own_trials * size
    lines = [
        shared_ref[member, main : main + own_trials, :size]
        for member in range(shared_ref.shape[0])
    ]
    trial_now = rows_product(eye_of(size), jnp.concatenate(lines, axis=0))
    inverse = damped_inverse(gram_of(trial_now) * gram_ref[...])
    put_neuron(trial_now, inverse, shared_ref, tensor_ref, raw_ref, sent_ref)


def neuron_body(shared_ref, trial_ref, inverse_ref, tensor_ref, raw_ref, sent_ref):
    put_neuron(trial_ref[...], inverse_ref[...], shared_ref, tensor_ref, raw_ref, sent_ref)


def reduce_body(got_ref, sent_ref):
    total = got_ref[0].astype(jnp.float32)
    for member in range(1, got_ref.shape[0]):
        total = total + got_ref[member].astype(jnp.float32)
    main = total.shape[0] - 2 * PART
    rounded = total[:main].astype(WIRE)
    halves = split(total[main : main + PART] + total[main + PART :])
    for member in range(sent_ref.shape[0]):
        sent_ref[member, :main, :] = rounded
        sent_ref[member, main:, :] = halves


def finish_body(neuron_count, plane_ref, got_ref, gram_ref, raw_ref, *outs):
    neuron_ref, neuron_gram_ref, trial_ref, trial_gram_ref, own_ref, sent_ref = outs
    size = raw_ref.shape[0]
    trial_count = trial_ref.shape[1]
    own_trials = own_ref.shape[0]
    total = got_ref[0].astype(jnp.float32)
    for member in range(1, got_ref.shape[0]):
        total = total + got_ref[member].astype(jnp.float32)
    main = own_trials * size
    small = total[main : main + PART] + total[main + PART :]
    raw_gram, terms = unpack_small(small, size, trial_count)
    diagonal = raw_gram * eye_of(size)
    down = 1.0 / jnp.sqrt(jnp.sum(diagonal, axis=1, keepdims=True) / neuron_count + tiny_eps)
    across = 1.0 / jnp.sqrt(jnp.sum(diagonal, axis=0, keepdims=True) / neuron_count + tiny_eps)
    neuron_ref[...] = raw_ref[...] * down
    neuron_gram = down * raw_gram * across
    neuron_gram_ref[...] = neuron_gram
    trial_now = product(damped_inverse(neuron_gram * gram_ref[...]), terms * down)
    trial_ref[...] = trial_now
    trial_gram_ref[...] = gram_of(trial_now)
    lane = lax.broadcasted_iota(jnp.int32, trial_now.shape, 1)
    row = lax.broadcasted_iota(jnp.int32, (own_trials, trial_count), 0)
    column = lax.broadcasted_iota(jnp.int32, (own_trials, trial_count), 1)
    chosen = (column == plane_ref[0] * own_trials + row).astype(jnp.float32)
    own_ref[...] = rows_product(chosen, trial_now)
    weighted = None
    for trial in range(own_trials):
        mine = lane == plane_ref[0] * own_trials + trial
        column = jnp.sum(jnp.where(mine, trial_now, 0.0), axis=1, keepdims=True)
        part = column * total[trial * size : (trial + 1) * size]
        weighted = part if weighted is None else weighted + part
    weighted = weighted * down
    for member in range(sent_ref.shape[0]):
        sent_ref[member] = weighted


def inverse_body(left_ref, right_ref, out_ref):
    out_ref[...] = damped_inverse(left_ref[...] * right_ref[...])


def time_of(planes, got_ref, inverse_ref):
    pieces = []
    for block in range(got_ref.shape[0] // planes):
        piece = got_ref[block * planes]
        for plane in range(1, planes):
            piece = piece + got_ref[block * planes + plane]
        pieces.append(piece)
    raw = product(inverse_ref[...], jnp.concatenate(pieces, axis=1))
    mean = jnp.sum(raw * raw, axis=1, keepdims=True) / raw.shape[1]
    return raw / jnp.sqrt(mean + tiny_eps)


def next_body(planes, got_ref, inverse_ref, tensor_ref, time_ref, sent_ref):
    time_now = time_of(planes, got_ref, inverse_ref)
    time_ref[...] = time_now
    put_projected(time_now, tensor_ref, sent_ref)


def gram_body(time_ref, gram_ref):
    gram_ref[...] = gram_of(time_ref[...])


def next_inverse_body(time_ref, trial_gram_ref, gram_ref, inverse_ref):
    gram = gram_of(time_ref[...])
    gram_ref[...] = gram
    inverse_ref[...] = damped_inverse(gram * trial_gram_ref[...])


def last_body(planes, place_ref, got_ref, inverse_ref, time_ref):
    time_now = time_of(planes, got_ref, inverse_ref)
    count = time_ref.shape[0]
    row = lax.broadcasted_iota(jnp.int32, (count, time_now.shape[1]), 0)
    column = lax.broadcasted_iota(jnp.int32, (count, time_now.shape[1]), 1)
    chosen = (column == place_ref[0] * count + row).astype(jnp.float32)
    time_ref[...] = rows_product(chosen, time_now)


def per_device(tensor, time_init, trial_init):
    own_trials, own_neurons, timepoints = tensor.shape
    components = time_init.shape[0]
    planes = lax.axis_size("x")
    short = ("y", "core")
    blocks = lax.axis_size(short)
    layers = lax.axis_size("z")
    neuron_count = own_neurons * blocks * layers
    trial_count = own_trials * planes
    width = timepoints // blocks
    main = own_trials * components
    plane = lax.axis_index("x").astype(jnp.int32).reshape(1)

    def shape(*dims, kind=jnp.float32):
        return jax.ShapeDtypeStruct(dims, kind)

    square = shape(components, components)
    neuron_outs = (
        shape(components, own_neurons),
        shape(blocks, main + 2 * PART, width, kind=WIRE),
    )
    shared = call(
        project_body,
        shape(planes, main + PART, own_neurons),
        time_init,
        trial_init.T,
        tensor,
    )
    shared = lax.all_to_all(shared, "x", 0, 0)
    time_gram = call(gram_body, square, time_init)
    raw, sent = call(first_neuron_body, neuron_outs, shared, time_gram, tensor)
    for sweep_index in range(SWEEPS):
        got = lax.all_to_all(sent, short, 0, 0)
        sent = call(reduce_body, shape(layers, main + 2 * PART, width, kind=WIRE), got)
        got = lax.all_to_all(sent, "z", 0, 0)
        neuron_now, neuron_gram, trial_now, trial_gram, own_trial, sent = call(
            lambda *refs: finish_body(neuron_count, *refs),
            (
                shape(components, own_neurons),
                square,
                shape(components, trial_count),
                square,
                shape(own_trials, components),
                shape(blocks * planes, components, width),
            ),
            plane,
            got,
            time_gram,
            raw,
            smem=(0,),
            slow=(0, 4) if sweep_index == SWEEPS - 1 else (),
        )
        got = lax.all_to_all(sent, short + ("x",), 0, 0)
        inverse = call(inverse_body, square, neuron_gram, trial_gram)
        if sweep_index == SWEEPS - 1:
            place = lax.axis_index(("z", "y", "core", "x")).astype(jnp.int32).reshape(1)
            time_out = call(
                lambda *refs: last_body(planes, *refs),
                shape(timepoints // (layers * blocks * planes), components),
                place,
                got,
                inverse,
                smem=(0,),
                slow=(0,),
            )
            break
        time_now, shared = call(
            lambda *refs: next_body(planes, *refs),
            (shape(components, timepoints), shape(planes, main, own_neurons)),
            got,
            inverse,
            tensor,
        )
        shared = lax.all_to_all(shared, "x", 0, 0)
        time_gram, inverse = call(next_inverse_body, (square, square), time_now, trial_gram)
        raw, sent = call(neuron_body, neuron_outs, shared, trial_now, inverse, tensor)
    return (neuron_now, time_out.T, own_trial.T)


def solution(mesh):
    neuron, trial = mesh.shape["neuron"], mesh.shape["trial"]
    layers = max(neuron // 8, 1)
    fine = Mesh(
        mesh.devices.reshape(layers, neuron // layers // 2, 2, trial), ("z", "y", "core", "x")
    )
    rows = ("z", "y", "core")
    return jax.shard_map(
        per_device,
        mesh=fine,
        in_specs=(P("x", rows, None), P(), P(None, "x")),
        out_specs=(P(None, rows), P(None, rows + ("x",)), P(None, "x")),
        check_vma=False,
    )
```

```python
import jax
import jax.numpy as jnp
from jax import lax
from jax.experimental import pallas as pl
from jax.experimental.pallas import tpu as pltpu
from jax.sharding import Mesh, PartitionSpec as P

SWEEPS = 2


ridge_share = 0.1
tiny_eps = 1e-06
EXACT = lax.Precision.HIGHEST
PART = 8
WIRE = jnp.bfloat16


def gram_of(matrix):
    return lax.dot_general(
        matrix,
        matrix,
        (((1,), (1,)), ((), ())),
        precision=EXACT,
        preferred_element_type=jnp.float32,
    )


def product(left, right):
    return lax.dot_general(
        left,
        right,
        (((1,), (0,)), ((), ())),
        precision=EXACT,
        preferred_element_type=jnp.float32,
    )


def rows_product(left, right):
    return lax.dot_general(
        left,
        right,
        (((1,), (1,)), ((), ())),
        precision=EXACT,
        preferred_element_type=jnp.float32,
    )


def split(values):
    high = values.astype(WIRE).astype(jnp.float32)
    return jnp.concatenate([high, values - high], axis=0).astype(WIRE)


def eye_of(size):
    rows = lax.broadcasted_iota(jnp.int32, (size, size), 0)
    cols = lax.broadcasted_iota(jnp.int32, (size, size), 1)
    return (rows == cols).astype(jnp.float32)


def damped_inverse(system):
    size = system.shape[0]
    eye = eye_of(size)
    trace = jnp.sum(jnp.sum(system * eye, axis=1, keepdims=True), axis=0, keepdims=True)
    share = size / trace
    both = jnp.concatenate([system * share + ridge_share * eye, eye], axis=1)
    row = lax.broadcasted_iota(jnp.int32, both.shape, 0)
    for step in range(0, size, 2):
        first = jnp.broadcast_to(both[:, step : step + 1], both.shape)
        second = jnp.broadcast_to(both[:, step + 1 : step + 2], both.shape)
        upper, lower = both[step : step + 1], both[step + 1 : step + 2]
        p00, p01 = first[step : step + 1], second[step : step + 1]
        p10, p11 = first[step + 1 : step + 2], second[step + 1 : step + 2]
        over = 1.0 / (p00 * p11 - p01 * p10)
        new_upper = (p11 * upper - p01 * lower) * over
        new_lower = (p00 * lower - p10 * upper) * over
        cleared = both - first * new_upper - second * new_lower
        both = jnp.where(row == step, new_upper, jnp.where(row == step + 1, new_lower, cleared))
    return both[:, size:] * share


def pack_small(gram, terms):
    size = gram.shape[0]
    pieces = []
    for start in range(0, size, PART):
        pieces.append(gram[start : start + PART, start:])
    for start in range(0, size, PART):
        pieces.append(terms[start : start + PART])
    used = sum(piece.shape[1] for piece in pieces)
    pieces.append(jnp.zeros((PART, 128 - used), jnp.float32))
    return jnp.concatenate(pieces, axis=1)


def unpack_small(tile, size, count):
    rows, place = [], 0
    for start in range(0, size, PART):
        piece = tile[:, place : place + size - start]
        place += size - start
        if start:
            piece = jnp.concatenate([jnp.zeros((PART, start), jnp.float32), piece], axis=1)
        rows.append(piece)
    upper = jnp.concatenate(rows, axis=0)
    terms = []
    for start in range(0, size, PART):
        terms.append(tile[:, place : place + count])
        place += count
    row_part = lax.broadcasted_iota(jnp.int32, (size, size), 0) // PART
    col_part = lax.broadcasted_iota(jnp.int32, (size, size), 1) // PART
    return jnp.where(col_part >= row_part, upper, upper.T), jnp.concatenate(terms, axis=0)


def call(body, outs, *args, away=(), slow=()):
    single = not isinstance(outs, tuple)
    listed = (outs,) if single else outs
    args = [
        arg if place in away else pltpu.with_memory_space_constraint(arg, pltpu.VMEM)
        for place, arg in enumerate(args)
    ]
    shapes = tuple(
        out if place in slow else pltpu.VMEM(out.shape, out.dtype)
        for place, out in enumerate(listed)
    )
    result = pl.pallas_call(
        body,
        out_shape=shapes,
        in_specs=[pl.BlockSpec(memory_space=pltpu.VMEM) for _ in args],
        out_specs=tuple(pl.BlockSpec(memory_space=pltpu.VMEM) for _ in listed),
    )(*args)
    return result[0] if single else result


def put_projected(time_now, tensor_ref, sent_ref):
    rounded = time_now.astype(jnp.bfloat16)
    size = time_now.shape[0]
    for trial in range(tensor_ref.shape[0]):
        projected = lax.dot_general(
            rounded,
            tensor_ref[trial],
            (((1,), (1,)), ((), ())),
            preferred_element_type=jnp.float32,
        )
        for member in range(sent_ref.shape[0]):
            sent_ref[member, trial * size : (trial + 1) * size, :] = projected


def project_body(time_ref, trial_ref, tensor_ref, sent_ref):
    put_projected(time_ref[...], tensor_ref, sent_ref)
    count, size = trial_ref.shape
    lanes = sent_ref.shape[2]
    tile = jnp.concatenate([trial_ref[...], jnp.zeros((PART - count, size), jnp.float32)], axis=0)
    tile = jnp.concatenate([tile, jnp.zeros((PART, lanes - size), jnp.float32)], axis=1)
    for member in range(sent_ref.shape[0]):
        sent_ref[member, count * size :, :] = tile


def put_neuron(trial_now, inverse, shared_ref, tensor_ref, raw_ref, sent_ref):
    size, trial_count = trial_now.shape
    own_trials = tensor_ref.shape[0]
    terms = []
    projected = []
    for trial in range(trial_count):
        start = trial % own_trials * size
        projected.append(shared_ref[trial // own_trials, start : start + size, :])
    neuron_terms = trial_now[:, 0:1] * projected[0]
    for trial in range(1, trial_count):
        neuron_terms = neuron_terms + trial_now[:, trial : trial + 1] * projected[trial]
    raw = product(inverse, neuron_terms)
    raw_ref[...] = raw
    lane = lax.broadcasted_iota(jnp.int32, (size, trial_count), 1)
    terms = jnp.zeros((size, trial_count), jnp.float32)
    for trial in range(trial_count):
        one = jnp.sum(raw * projected[trial], axis=1, keepdims=True)
        terms = jnp.where(lane == trial, one, terms)
    small = split(pack_small(gram_of(raw), terms))
    members, rows, width = sent_ref.shape
    blocks = tensor_ref.shape[2] // width
    rounded = raw.astype(jnp.bfloat16)
    for trial in range(own_trials):
        partial = jnp.dot(rounded, tensor_ref[trial], preferred_element_type=jnp.float32)
        partial = partial.astype(WIRE)
        for member in range(members):
            start = member % blocks * width
            sent_ref[member, trial * size : (trial + 1) * size, :] = partial[
                :, start : start + width
            ]
    for member in range(members):
        sent_ref[member, own_trials * size :, :] = small


def first_neuron_body(shared_ref, gram_ref, tensor_ref, raw_ref, sent_ref):
    own_trials = tensor_ref.shape[0]
    size = raw_ref.shape[0]
    main = own_trials * size
    lines = [
        shared_ref[member, main : main + own_trials, :size]
        for member in range(shared_ref.shape[0])
    ]
    trial_now = rows_product(eye_of(size), jnp.concatenate(lines, axis=0))
    inverse = damped_inverse(gram_of(trial_now) * gram_ref[...])
    put_neuron(trial_now, inverse, shared_ref, tensor_ref, raw_ref, sent_ref)


def neuron_body(shared_ref, trial_ref, inverse_ref, tensor_ref, raw_ref, sent_ref):
    put_neuron(trial_ref[...], inverse_ref[...], shared_ref, tensor_ref, raw_ref, sent_ref)


def reduce_body(got_ref, sent_ref):
    total = got_ref[0].astype(jnp.float32)
    for member in range(1, got_ref.shape[0]):
        total = total + got_ref[member].astype(jnp.float32)
    main = total.shape[0] - 2 * PART
    rounded = total[:main].astype(WIRE)
    halves = split(total[main : main + PART] + total[main + PART :])
    for member in range(sent_ref.shape[0]):
        sent_ref[member, :main, :] = rounded
        sent_ref[member, main:, :] = halves


def finish_body(neuron_count, got_ref, gram_ref, raw_ref, *outs):
    neuron_ref, neuron_gram_ref, trial_ref, trial_gram_ref, own_ref, sent_ref = outs
    size = raw_ref.shape[0]
    trial_count = trial_ref.shape[1]
    own_trials = own_ref.shape[0]
    plane = lax.axis_index("x")
    total = got_ref[0].astype(jnp.float32)
    for member in range(1, got_ref.shape[0]):
        total = total + got_ref[member].astype(jnp.float32)
    main = own_trials * size
    small = total[main : main + PART] + total[main + PART :]
    raw_gram, terms = unpack_small(small, size, trial_count)
    diagonal = raw_gram * eye_of(size)
    down = 1.0 / jnp.sqrt(jnp.sum(diagonal, axis=1, keepdims=True) / neuron_count + tiny_eps)
    across = 1.0 / jnp.sqrt(jnp.sum(diagonal, axis=0, keepdims=True) / neuron_count + tiny_eps)
    neuron_ref[...] = raw_ref[...] * down
    neuron_gram = down * raw_gram * across
    neuron_gram_ref[...] = neuron_gram
    trial_now = product(damped_inverse(neuron_gram * gram_ref[...]), terms * down)
    trial_ref[...] = trial_now
    trial_gram_ref[...] = gram_of(trial_now)
    lane = lax.broadcasted_iota(jnp.int32, trial_now.shape, 1)
    row = lax.broadcasted_iota(jnp.int32, (own_trials, trial_count), 0)
    column = lax.broadcasted_iota(jnp.int32, (own_trials, trial_count), 1)
    chosen = (column == plane * own_trials + row).astype(jnp.float32)
    own_ref[...] = rows_product(chosen, trial_now)
    weighted = None
    for trial in range(own_trials):
        mine = lane == plane * own_trials + trial
        column = jnp.sum(jnp.where(mine, trial_now, 0.0), axis=1, keepdims=True)
        part = column * total[trial * size : (trial + 1) * size]
        weighted = part if weighted is None else weighted + part
    weighted = weighted * down
    for member in range(sent_ref.shape[0]):
        sent_ref[member] = weighted


def inverse_body(left_ref, right_ref, out_ref):
    out_ref[...] = damped_inverse(left_ref[...] * right_ref[...])


def time_of(planes, got_ref, inverse_ref):
    pieces = []
    for block in range(got_ref.shape[0] // planes):
        piece = got_ref[block * planes]
        for plane in range(1, planes):
            piece = piece + got_ref[block * planes + plane]
        pieces.append(piece)
    raw = product(inverse_ref[...], jnp.concatenate(pieces, axis=1))
    mean = jnp.sum(raw * raw, axis=1, keepdims=True) / raw.shape[1]
    return raw / jnp.sqrt(mean + tiny_eps)


def next_body(planes, got_ref, inverse_ref, tensor_ref, time_ref, sent_ref):
    time_now = time_of(planes, got_ref, inverse_ref)
    time_ref[...] = time_now
    put_projected(time_now, tensor_ref, sent_ref)


def gram_body(time_ref, gram_ref):
    gram_ref[...] = gram_of(time_ref[...])


def next_inverse_body(time_ref, trial_gram_ref, gram_ref, inverse_ref):
    gram = gram_of(time_ref[...])
    gram_ref[...] = gram
    inverse_ref[...] = damped_inverse(gram * trial_gram_ref[...])


def last_body(planes, got_ref, inverse_ref, time_ref):
    time_now = time_of(planes, got_ref, inverse_ref)
    count = time_ref.shape[0]
    row = lax.broadcasted_iota(jnp.int32, (count, time_now.shape[1]), 0)
    column = lax.broadcasted_iota(jnp.int32, (count, time_now.shape[1]), 1)
    chosen = (column == lax.axis_index(("z", "pair", "y", "core", "x")) * count + row).astype(jnp.float32)
    time_ref[...] = rows_product(chosen, time_now)


def per_device(tensor, time_init, trial_init):
    own_trials, own_neurons, timepoints = tensor.shape
    components = time_init.shape[0]
    planes = lax.axis_size("x")
    short = ("y", "core")
    near = ("pair",) + short
    blocks, layers = lax.axis_size(short), lax.axis_size("z")
    twins = lax.axis_size("pair")
    neuron_count = own_neurons * blocks * twins * layers
    trial_count = own_trials * planes
    width = timepoints // blocks
    main = own_trials * components

    def shape(*dims, kind=jnp.float32):
        return jax.ShapeDtypeStruct(dims, kind)

    square = shape(components, components)
    neuron_outs = (
        shape(components, own_neurons),
        shape(twins * blocks, main + 2 * PART, width, kind=WIRE),
    )
    shared = call(
        project_body,
        shape(planes, main + PART, own_neurons),
        time_init,
        trial_init.T,
        tensor,
        away=(0, 1, 2),
    )
    shared = lax.all_to_all(shared, "x", 0, 0)
    time_gram = call(gram_body, square, time_init)
    raw, sent = call(first_neuron_body, neuron_outs, shared, time_gram, tensor)
    for sweep_index in range(SWEEPS):
        got = lax.all_to_all(sent, near, 0, 0)
        sent = call(reduce_body, shape(layers, main + 2 * PART, width, kind=WIRE), got)
        got = lax.all_to_all(sent, "z", 0, 0)
        neuron_now, neuron_gram, trial_now, trial_gram, own_trial, sent = call(
            lambda *refs: finish_body(neuron_count, *refs),
            (
                shape(components, own_neurons),
                square,
                shape(components, trial_count),
                square,
                shape(own_trials, components),
                shape(blocks * planes, components, width),
            ),
            got,
            time_gram,
            raw,
            slow=(0, 4) if sweep_index == SWEEPS - 1 else (),
        )
        got = lax.all_to_all(sent, short + ("x",), 0, 0)
        inverse = call(inverse_body, square, neuron_gram, trial_gram)
        if sweep_index == SWEEPS - 1:
            time_out = call(
                lambda *refs: last_body(planes, *refs),
                shape(timepoints // (layers * twins * blocks * planes), components),
                got,
                inverse,
                slow=(0,),
            )
            break
        time_now, shared = call(
            lambda *refs: next_body(planes, *refs),
            (shape(components, timepoints), shape(planes, main, own_neurons)),
            got,
            inverse,
            tensor,
        )
        shared = lax.all_to_all(shared, "x", 0, 0)
        time_gram, inverse = call(next_inverse_body, (square, square), time_now, trial_gram)
        raw, sent = call(neuron_body, neuron_outs, shared, trial_now, inverse, tensor)
    return (neuron_now, time_out.T, own_trial.T)


def solution(mesh):
    neuron, trial = mesh.shape["neuron"], mesh.shape["trial"]
    layers = neuron // 16
    fine = Mesh(
        mesh.devices.reshape(layers, 2, 4, 2, trial), ("z", "pair", "y", "core", "x")
    )
    rows = ("z", "pair", "y", "core")
    return jax.shard_map(
        per_device,
        mesh=fine,
        in_specs=(P("x", rows, None), P(), P(None, "x")),
        out_specs=(P(None, rows), P(None, rows + ("x",)), P(None, "x")),
        check_vma=False,
    )
```

```python
import jax
import jax.numpy as jnp
from jax import lax
from jax.experimental import pallas as pl
from jax.experimental.pallas import tpu as pltpu
from jax.sharding import Mesh, PartitionSpec as P

SWEEPS = 2


ridge_share = 0.1
tiny_eps = 1e-06
EXACT = lax.Precision.HIGHEST
PART = 8
WIRE = jnp.bfloat16


def gram_of(matrix):
    return lax.dot_general(
        matrix,
        matrix,
        (((1,), (1,)), ((), ())),
        precision=EXACT,
        preferred_element_type=jnp.float32,
    )


def product(left, right):
    return lax.dot_general(
        left,
        right,
        (((1,), (0,)), ((), ())),
        precision=EXACT,
        preferred_element_type=jnp.float32,
    )


def rows_product(left, right):
    return lax.dot_general(
        left,
        right,
        (((1,), (1,)), ((), ())),
        precision=EXACT,
        preferred_element_type=jnp.float32,
    )


def split(values):
    high = values.astype(WIRE).astype(jnp.float32)
    return jnp.concatenate([high, values - high], axis=0).astype(WIRE)


def eye_of(size):
    rows = lax.broadcasted_iota(jnp.int32, (size, size), 0)
    cols = lax.broadcasted_iota(jnp.int32, (size, size), 1)
    return (rows == cols).astype(jnp.float32)


def damped_inverse(system):
    size = system.shape[0]
    eye = eye_of(size)
    trace = jnp.sum(jnp.sum(system * eye, axis=1, keepdims=True), axis=0, keepdims=True)
    share = size / trace
    both = jnp.concatenate([system * share + ridge_share * eye, eye], axis=1)
    row = lax.broadcasted_iota(jnp.int32, both.shape, 0)
    for step in range(0, size, 2):
        first = jnp.broadcast_to(both[:, step : step + 1], both.shape)
        second = jnp.broadcast_to(both[:, step + 1 : step + 2], both.shape)
        upper, lower = both[step : step + 1], both[step + 1 : step + 2]
        p00, p01 = first[step : step + 1], second[step : step + 1]
        p10, p11 = first[step + 1 : step + 2], second[step + 1 : step + 2]
        over = 1.0 / (p00 * p11 - p01 * p10)
        new_upper = (p11 * upper - p01 * lower) * over
        new_lower = (p00 * lower - p10 * upper) * over
        cleared = both - first * new_upper - second * new_lower
        both = jnp.where(row == step, new_upper, jnp.where(row == step + 1, new_lower, cleared))
    return both[:, size:] * share


def pack_small(gram, terms):
    size = gram.shape[0]
    pieces = []
    for start in range(0, size, PART):
        pieces.append(gram[start : start + PART, start:])
    for start in range(0, size, PART):
        pieces.append(terms[start : start + PART])
    used = sum(piece.shape[1] for piece in pieces)
    pieces.append(jnp.zeros((PART, 128 - used), jnp.float32))
    return jnp.concatenate(pieces, axis=1)


def unpack_small(tile, size, count):
    rows, place = [], 0
    for start in range(0, size, PART):
        piece = tile[:, place : place + size - start]
        place += size - start
        if start:
            piece = jnp.concatenate([jnp.zeros((PART, start), jnp.float32), piece], axis=1)
        rows.append(piece)
    upper = jnp.concatenate(rows, axis=0)
    terms = []
    for start in range(0, size, PART):
        terms.append(tile[:, place : place + count])
        place += count
    row_part = lax.broadcasted_iota(jnp.int32, (size, size), 0) // PART
    col_part = lax.broadcasted_iota(jnp.int32, (size, size), 1) // PART
    return jnp.where(col_part >= row_part, upper, upper.T), jnp.concatenate(terms, axis=0)


def call(body, outs, *args, away=(), slow=()):
    single = not isinstance(outs, tuple)
    listed = (outs,) if single else outs
    args = [
        arg if place in away else pltpu.with_memory_space_constraint(arg, pltpu.VMEM)
        for place, arg in enumerate(args)
    ]
    shapes = tuple(
        out if place in slow else pltpu.VMEM(out.shape, out.dtype)
        for place, out in enumerate(listed)
    )
    result = pl.pallas_call(
        body,
        out_shape=shapes,
        in_specs=[pl.BlockSpec(memory_space=pltpu.VMEM) for _ in args],
        out_specs=tuple(pl.BlockSpec(memory_space=pltpu.VMEM) for _ in listed),
    )(*args)
    return result[0] if single else result


def put_projected(time_now, tensor_ref, sent_ref):
    rounded = time_now.astype(jnp.bfloat16)
    size = time_now.shape[0]
    for trial in range(tensor_ref.shape[0]):
        projected = lax.dot_general(
            rounded,
            tensor_ref[trial],
            (((1,), (1,)), ((), ())),
            preferred_element_type=jnp.float32,
        )
        for member in range(sent_ref.shape[0]):
            sent_ref[member, trial * size : (trial + 1) * size, :] = projected


def project_body(time_ref, trial_ref, tensor_ref, sent_ref):
    put_projected(time_ref[...], tensor_ref, sent_ref)
    count, size = trial_ref.shape
    lanes = sent_ref.shape[2]
    tile = jnp.concatenate([trial_ref[...], jnp.zeros((PART - count, size), jnp.float32)], axis=0)
    tile = jnp.concatenate([tile, jnp.zeros((PART, lanes - size), jnp.float32)], axis=1)
    for member in range(sent_ref.shape[0]):
        sent_ref[member, count * size :, :] = tile


def put_neuron(trial_now, inverse, shared_ref, tensor_ref, raw_ref, sent_ref):
    size, trial_count = trial_now.shape
    own_trials = tensor_ref.shape[0]
    terms = []
    projected = []
    for trial in range(trial_count):
        start = trial % own_trials * size
        projected.append(shared_ref[trial // own_trials, start : start + size, :])
    neuron_terms = trial_now[:, 0:1] * projected[0]
    for trial in range(1, trial_count):
        neuron_terms = neuron_terms + trial_now[:, trial : trial + 1] * projected[trial]
    raw = product(inverse, neuron_terms)
    raw_ref[...] = raw
    lane = lax.broadcasted_iota(jnp.int32, (size, trial_count), 1)
    terms = jnp.zeros((size, trial_count), jnp.float32)
    for trial in range(trial_count):
        one = jnp.sum(raw * projected[trial], axis=1, keepdims=True)
        terms = jnp.where(lane == trial, one, terms)
    small = split(pack_small(gram_of(raw), terms))
    members, _, lanes = sent_ref.shape
    blocks = tensor_ref.shape[2] // lanes
    low = lax.broadcasted_iota(jnp.int32, (size, lanes), 1) < lanes // 2
    rounded = raw.astype(jnp.bfloat16)
    first = jnp.dot(rounded, tensor_ref[0], preferred_element_type=jnp.float32)
    second = jnp.dot(rounded, tensor_ref[1], preferred_element_type=jnp.float32)
    for block in range(blocks):
        start = block * lanes
        one = first[:, start : start + lanes]
        two = pltpu.roll(second[:, start : start + lanes], lanes // 2, 1)
        sent_ref[block, :size, :] = jnp.where(low, one, two).astype(WIRE)
        sent_ref[blocks + block, :size, :] = jnp.where(low, two, one).astype(WIRE)
    for member in range(members):
        sent_ref[member, size:, :] = small


def first_neuron_body(shared_ref, gram_ref, tensor_ref, raw_ref, sent_ref):
    own_trials = tensor_ref.shape[0]
    size = raw_ref.shape[0]
    main = own_trials * size
    lines = [
        shared_ref[member, main : main + own_trials, :size]
        for member in range(shared_ref.shape[0])
    ]
    trial_now = rows_product(eye_of(size), jnp.concatenate(lines, axis=0))
    inverse = damped_inverse(gram_of(trial_now) * gram_ref[...])
    put_neuron(trial_now, inverse, shared_ref, tensor_ref, raw_ref, sent_ref)


def neuron_body(shared_ref, trial_ref, inverse_ref, tensor_ref, raw_ref, sent_ref):
    put_neuron(trial_ref[...], inverse_ref[...], shared_ref, tensor_ref, raw_ref, sent_ref)


def reduce_body(got_ref, sent_ref):
    total = got_ref[0].astype(jnp.float32)
    for member in range(1, got_ref.shape[0]):
        total = total + got_ref[member].astype(jnp.float32)
    main = total.shape[0] - 2 * PART
    rounded = total[:main].astype(WIRE)
    halves = split(total[main : main + PART] + total[main + PART :])
    for member in range(sent_ref.shape[0]):
        sent_ref[member, :main, :] = rounded
        sent_ref[member, main:, :] = halves


def finish_body(neuron_count, got_ref, gram_ref, raw_ref, *outs):
    neuron_ref, neuron_gram_ref, trial_ref, trial_gram_ref, own_ref, sent_ref = outs
    size = raw_ref.shape[0]
    trial_count = trial_ref.shape[1]
    own_trials = own_ref.shape[0]
    plane = lax.axis_index("x")
    total = got_ref[0].astype(jnp.float32)
    for member in range(1, got_ref.shape[0]):
        total = total + got_ref[member].astype(jnp.float32)
    small = total[size : size + PART] + total[size + PART :]
    raw_gram, terms = unpack_small(small, size, trial_count)
    diagonal = raw_gram * eye_of(size)
    down = 1.0 / jnp.sqrt(jnp.sum(diagonal, axis=1, keepdims=True) / neuron_count + tiny_eps)
    across = 1.0 / jnp.sqrt(jnp.sum(diagonal, axis=0, keepdims=True) / neuron_count + tiny_eps)
    neuron_ref[...] = raw_ref[...] * down
    neuron_gram = down * raw_gram * across
    neuron_gram_ref[...] = neuron_gram
    trial_now = product(damped_inverse(neuron_gram * gram_ref[...]), terms * down)
    trial_ref[...] = trial_now
    trial_gram_ref[...] = gram_of(trial_now)
    lane = lax.broadcasted_iota(jnp.int32, trial_now.shape, 1)
    row = lax.broadcasted_iota(jnp.int32, (own_trials, trial_count), 0)
    column = lax.broadcasted_iota(jnp.int32, (own_trials, trial_count), 1)
    chosen = (column == plane * own_trials + row).astype(jnp.float32)
    own_ref[...] = rows_product(chosen, trial_now)
    columns = []
    for trial in range(own_trials):
        mine = lane == plane * own_trials + trial
        columns.append(jnp.sum(jnp.where(mine, trial_now, 0.0), axis=1, keepdims=True))
    lanes = total.shape[1]
    low = lax.broadcasted_iota(jnp.int32, (size, lanes), 1) < lanes // 2
    same = low == (lax.axis_index("pair") == 0)
    weighted = jnp.where(same, columns[0], columns[1]) * down * total[:size]
    weighted = weighted + pltpu.roll(weighted, lanes // 2, 1)
    half = size // 2
    weighted = jnp.where(low[:half], weighted[:half], weighted[half:])
    for member in range(sent_ref.shape[0]):
        sent_ref[member] = weighted


def sum_body(got_ref, sent_ref):
    total = got_ref[0]
    for member in range(1, got_ref.shape[0]):
        total = total + got_ref[member]
    for member in range(sent_ref.shape[0]):
        sent_ref[member] = total


def inverse_body(left_ref, right_ref, out_ref):
    out_ref[...] = damped_inverse(left_ref[...] * right_ref[...])


def time_of(got_ref, inverse_ref):
    members, half, lanes = got_ref.shape
    low = lax.broadcasted_iota(jnp.int32, (half, lanes), 1) < lanes // 2
    pieces = []
    for block in range(members // 2):
        one, two = got_ref[block], got_ref[members // 2 + block]
        upper = jnp.where(low, one, pltpu.roll(two, lanes // 2, 1))
        lower = jnp.where(low, pltpu.roll(one, lanes // 2, 1), two)
        pieces.append(jnp.concatenate([upper, lower], axis=0))
    raw = product(inverse_ref[...], jnp.concatenate(pieces, axis=1))
    mean = jnp.sum(raw * raw, axis=1, keepdims=True) / raw.shape[1]
    return raw / jnp.sqrt(mean + tiny_eps)


def next_body(got_ref, inverse_ref, tensor_ref, time_ref, sent_ref):
    time_now = time_of(got_ref, inverse_ref)
    time_ref[...] = time_now
    put_projected(time_now, tensor_ref, sent_ref)


def gram_body(time_ref, gram_ref):
    gram_ref[...] = gram_of(time_ref[...])


def next_inverse_body(time_ref, trial_gram_ref, gram_ref, inverse_ref):
    gram = gram_of(time_ref[...])
    gram_ref[...] = gram
    inverse_ref[...] = damped_inverse(gram * trial_gram_ref[...])


def last_body(got_ref, inverse_ref, time_ref):
    time_now = time_of(got_ref, inverse_ref)
    count = time_ref.shape[0]
    row = lax.broadcasted_iota(jnp.int32, (count, time_now.shape[1]), 0)
    column = lax.broadcasted_iota(jnp.int32, (count, time_now.shape[1]), 1)
    chosen = (column == lax.axis_index(("z", "pair", "y", "core", "x")) * count + row).astype(jnp.float32)
    time_ref[...] = rows_product(chosen, time_now)


def per_device(tensor, time_init, trial_init):
    own_trials, own_neurons, timepoints = tensor.shape
    components = time_init.shape[0]
    planes = lax.axis_size("x")
    short = ("y", "core")
    near = ("pair",) + short
    blocks, layers = lax.axis_size(short), lax.axis_size("z")
    twins = lax.axis_size("pair")
    neuron_count = own_neurons * blocks * twins * layers
    trial_count = own_trials * planes
    lanes = timepoints // blocks
    main = own_trials * components

    def shape(*dims, kind=jnp.float32):
        return jax.ShapeDtypeStruct(dims, kind)

    square = shape(components, components)
    neuron_outs = (
        shape(components, own_neurons),
        shape(twins * blocks, components + 2 * PART, lanes, kind=WIRE),
    )
    shared = call(
        project_body,
        shape(planes, main + PART, own_neurons),
        time_init,
        trial_init.T,
        tensor,
        away=(0, 1, 2),
    )
    shared = lax.all_to_all(shared, "x", 0, 0)
    time_gram = call(gram_body, square, time_init)
    raw, sent = call(first_neuron_body, neuron_outs, shared, time_gram, tensor)
    for sweep_index in range(SWEEPS):
        got = lax.all_to_all(sent, near, 0, 0)
        sent = call(reduce_body, shape(layers, components + 2 * PART, lanes, kind=WIRE), got)
        got = lax.all_to_all(sent, "z", 0, 0)
        neuron_now, neuron_gram, trial_now, trial_gram, own_trial, sent = call(
            lambda *refs: finish_body(neuron_count, *refs),
            (
                shape(components, own_neurons),
                square,
                shape(components, trial_count),
                square,
                shape(own_trials, components),
                shape(planes, components // 2, lanes),
            ),
            got,
            time_gram,
            raw,
            slow=(0, 4) if sweep_index == SWEEPS - 1 else (),
        )
        got = lax.all_to_all(sent, "x", 0, 0)
        sent = call(sum_body, shape(twins * blocks, components // 2, lanes), got)
        got = lax.all_to_all(sent, near, 0, 0)
        inverse = call(inverse_body, square, neuron_gram, trial_gram)
        if sweep_index == SWEEPS - 1:
            time_out = call(
                last_body,
                shape(timepoints // (layers * twins * blocks * planes), components),
                got,
                inverse,
                slow=(0,),
            )
            break
        time_now, shared = call(
            next_body,
            (shape(components, timepoints), shape(planes, main, own_neurons)),
            got,
            inverse,
            tensor,
        )
        shared = lax.all_to_all(shared, "x", 0, 0)
        time_gram, inverse = call(next_inverse_body, (square, square), time_now, trial_gram)
        raw, sent = call(neuron_body, neuron_outs, shared, trial_now, inverse, tensor)
    return (neuron_now, time_out.T, own_trial.T)


def solution(mesh):
    neuron, trial = mesh.shape["neuron"], mesh.shape["trial"]
    layers = neuron // 16
    fine = Mesh(
        mesh.devices.reshape(layers, 2, 4, 2, trial), ("z", "pair", "y", "core", "x")
    )
    rows = ("z", "pair", "y", "core")
    return jax.shard_map(
        per_device,
        mesh=fine,
        in_specs=(P("x", rows, None), P(), P(None, "x")),
        out_specs=(P(None, rows), P(None, rows + ("x",)), P(None, "x")),
        check_vma=False,
    )
```

```python
import jax
import jax.numpy as jnp
from jax import lax
from jax.experimental import pallas as pl
from jax.experimental.pallas import tpu as pltpu
from jax.sharding import Mesh, PartitionSpec as P

SWEEPS = 2


ridge_share = 0.1
tiny_eps = 1e-06
EXACT = lax.Precision.HIGHEST
PART = 8
WIRE = jnp.bfloat16


def gram_of(matrix):
    return lax.dot_general(
        matrix,
        matrix,
        (((1,), (1,)), ((), ())),
        precision=EXACT,
        preferred_element_type=jnp.float32,
    )


def product(left, right):
    return lax.dot_general(
        left,
        right,
        (((1,), (0,)), ((), ())),
        precision=EXACT,
        preferred_element_type=jnp.float32,
    )


def rows_product(left, right):
    return lax.dot_general(
        left,
        right,
        (((1,), (1,)), ((), ())),
        precision=EXACT,
        preferred_element_type=jnp.float32,
    )


def split(values):
    high = values.astype(WIRE).astype(jnp.float32)
    return jnp.concatenate([high, values - high], axis=0).astype(WIRE)


def eye_of(size):
    rows = lax.broadcasted_iota(jnp.int32, (size, size), 0)
    cols = lax.broadcasted_iota(jnp.int32, (size, size), 1)
    return (rows == cols).astype(jnp.float32)


def damped_inverse(system):
    size = system.shape[0]
    eye = eye_of(size)
    trace = jnp.sum(jnp.sum(system * eye, axis=1, keepdims=True), axis=0, keepdims=True)
    share = size / trace
    both = jnp.concatenate([system * share + ridge_share * eye, eye], axis=1)
    row = lax.broadcasted_iota(jnp.int32, both.shape, 0)

    def pivots(step):
        if step >= size:
            return []
        return [
            jnp.broadcast_to(both[:, place : place + 1], both.shape) for place in (step, step + 1)
        ]

    ahead = [pivots(0), pivots(2)]
    for step in range(0, size, 2):
        first, second = ahead[0]
        p00, p01 = first[step : step + 1], second[step : step + 1]
        p10, p11 = first[step + 1 : step + 2], second[step + 1 : step + 2]
        over = 1.0 / (p00 * p11 - p01 * p10)
        p00, p01, p10, p11 = p00 * over, p01 * over, p10 * over, p11 * over

        def cleared(matrix):
            upper, lower = matrix[step : step + 1], matrix[step + 1 : step + 2]
            new_upper = p11 * upper - p01 * lower
            new_lower = p00 * lower - p10 * upper
            rest = matrix - first * new_upper - second * new_lower
            return jnp.where(row == step, new_upper, jnp.where(row == step + 1, new_lower, rest))

        ahead = [[cleared(one) for one in ahead[1]], [cleared(one) for one in pivots(step + 4)]]
        both = cleared(both)
    return both[:, size:] * share


def pack_small(gram, terms):
    size = gram.shape[0]
    pieces = []
    for start in range(0, size, PART):
        pieces.append(gram[start : start + PART, start:])
    for start in range(0, size, PART):
        pieces.append(terms[start : start + PART])
    used = sum(piece.shape[1] for piece in pieces)
    pieces.append(jnp.zeros((PART, 128 - used), jnp.float32))
    return jnp.concatenate(pieces, axis=1)


def unpack_small(tile, size, count):
    rows, place = [], 0
    for start in range(0, size, PART):
        piece = tile[:, place : place + size - start]
        place += size - start
        if start:
            piece = jnp.concatenate([jnp.zeros((PART, start), jnp.float32), piece], axis=1)
        rows.append(piece)
    upper = jnp.concatenate(rows, axis=0)
    terms = []
    for start in range(0, size, PART):
        terms.append(tile[:, place : place + count])
        place += count
    row_part = lax.broadcasted_iota(jnp.int32, (size, size), 0) // PART
    col_part = lax.broadcasted_iota(jnp.int32, (size, size), 1) // PART
    return jnp.where(col_part >= row_part, upper, upper.T), jnp.concatenate(terms, axis=0)


def call(body, outs, *args, away=(), slow=()):
    single = not isinstance(outs, tuple)
    listed = (outs,) if single else outs
    args = [
        arg if place in away else pltpu.with_memory_space_constraint(arg, pltpu.VMEM)
        for place, arg in enumerate(args)
    ]
    shapes = tuple(
        out if place in slow else pltpu.VMEM(out.shape, out.dtype)
        for place, out in enumerate(listed)
    )
    result = pl.pallas_call(
        body,
        out_shape=shapes,
        in_specs=[pl.BlockSpec(memory_space=pltpu.VMEM) for _ in args],
        out_specs=tuple(pl.BlockSpec(memory_space=pltpu.VMEM) for _ in listed),
    )(*args)
    return result[0] if single else result


def put_projected(time_now, tensor_of, sent_ref):
    rounded = time_now.astype(jnp.bfloat16)
    size = time_now.shape[0]
    for trial in range(sent_ref.shape[1] // size):
        projected = lax.dot_general(
            rounded,
            tensor_of(trial),
            (((1,), (1,)), ((), ())),
            preferred_element_type=jnp.float32,
        )
        for member in range(sent_ref.shape[0]):
            sent_ref[member, trial * size : (trial + 1) * size, :] = projected


def project_body(time_hbm, trial_hbm, tensor_hbm, sent_ref, time_ref, trial_ref, tensor_ref, arrived):
    count, size = trial_ref.shape
    copies = [
        pltpu.make_async_copy(time_hbm, time_ref, arrived.at[0]),
        pltpu.make_async_copy(trial_hbm, trial_ref, arrived.at[1]),
    ]
    for trial in range(count):
        copies.append(
            pltpu.make_async_copy(tensor_hbm.at[trial], tensor_ref.at[trial], arrived.at[2 + trial])
        )
    for copy in copies:
        copy.start()
    copies[0].wait()

    def tensor_of(trial):
        copies[2 + trial].wait()
        return tensor_ref[trial]

    put_projected(time_ref[...], tensor_of, sent_ref)
    copies[1].wait()
    lanes = sent_ref.shape[2]
    tile = jnp.concatenate([trial_ref[...], jnp.zeros((PART - count, size), jnp.float32)], axis=0)
    tile = jnp.concatenate([tile, jnp.zeros((PART, lanes - size), jnp.float32)], axis=1)
    for member in range(sent_ref.shape[0]):
        sent_ref[member, count * size :, :] = tile


def project(out, time_init, trial_rows, tensor):
    return pl.pallas_call(
        project_body,
        out_shape=out,
        in_specs=[pl.BlockSpec(memory_space=pl.ANY) for _ in range(3)],
        out_specs=pl.BlockSpec(memory_space=pltpu.VMEM),
        scratch_shapes=[
            pltpu.VMEM(time_init.shape, time_init.dtype),
            pltpu.VMEM(trial_rows.shape, trial_rows.dtype),
            pltpu.VMEM(tensor.shape, tensor.dtype),
            pltpu.SemaphoreType.DMA((2 + tensor.shape[0],)),
        ],
    )(time_init, trial_rows, tensor)


def put_neuron(trial_now, inverse, shared_ref, tensor_ref, raw_ref, sent_ref):
    size, trial_count = trial_now.shape
    own_trials = tensor_ref.shape[0]
    terms = []
    projected = []
    for trial in range(trial_count):
        start = trial % own_trials * size
        projected.append(shared_ref[trial // own_trials, start : start + size, :])
    neuron_terms = trial_now[:, 0:1] * projected[0]
    for trial in range(1, trial_count):
        neuron_terms = neuron_terms + trial_now[:, trial : trial + 1] * projected[trial]
    raw = product(inverse, neuron_terms)
    raw_ref[...] = raw
    lane = lax.broadcasted_iota(jnp.int32, (size, trial_count), 1)
    terms = jnp.zeros((size, trial_count), jnp.float32)
    for trial in range(trial_count):
        one = jnp.sum(raw * projected[trial], axis=1, keepdims=True)
        terms = jnp.where(lane == trial, one, terms)
    small = split(pack_small(gram_of(raw), terms))
    members, _, lanes = sent_ref.shape
    blocks = tensor_ref.shape[2] // lanes
    low = lax.broadcasted_iota(jnp.int32, (size, lanes), 1) < lanes // 2
    rounded = raw.astype(jnp.bfloat16)
    first = jnp.dot(rounded, tensor_ref[0], preferred_element_type=jnp.float32)
    second = jnp.dot(rounded, tensor_ref[1], preferred_element_type=jnp.float32)
    for block in range(blocks):
        start = block * lanes
        one = first[:, start : start + lanes]
        two = pltpu.roll(second[:, start : start + lanes], lanes // 2, 1)
        sent_ref[block, :size, :] = jnp.where(low, one, two).astype(WIRE)
        sent_ref[blocks + block, :size, :] = jnp.where(low, two, one).astype(WIRE)
    for member in range(members):
        sent_ref[member, size:, :] = small


def first_neuron_body(shared_ref, gram_ref, tensor_ref, raw_ref, sent_ref):
    own_trials = tensor_ref.shape[0]
    size = raw_ref.shape[0]
    main = own_trials * size
    lines = [
        shared_ref[member, main : main + own_trials, :size]
        for member in range(shared_ref.shape[0])
    ]
    trial_now = rows_product(eye_of(size), jnp.concatenate(lines, axis=0))
    inverse = damped_inverse(gram_of(trial_now) * gram_ref[...])
    put_neuron(trial_now, inverse, shared_ref, tensor_ref, raw_ref, sent_ref)


def neuron_body(shared_ref, trial_ref, inverse_ref, tensor_ref, raw_ref, sent_ref):
    put_neuron(trial_ref[...], inverse_ref[...], shared_ref, tensor_ref, raw_ref, sent_ref)


def reduce_body(got_ref, sent_ref):
    total = got_ref[0].astype(jnp.float32)
    for member in range(1, got_ref.shape[0]):
        total = total + got_ref[member].astype(jnp.float32)
    main = total.shape[0] - 2 * PART
    rounded = total[:main].astype(WIRE)
    halves = split(total[main : main + PART] + total[main + PART :])
    for member in range(sent_ref.shape[0]):
        sent_ref[member, :main, :] = rounded
        sent_ref[member, main:, :] = halves


def finish_body(neuron_count, got_ref, gram_ref, raw_ref, *outs):
    neuron_ref, neuron_gram_ref, trial_ref, trial_gram_ref, own_ref, sent_ref = outs
    size = raw_ref.shape[0]
    trial_count = trial_ref.shape[1]
    own_trials = own_ref.shape[0]
    plane = lax.axis_index("x")
    total = got_ref[0].astype(jnp.float32)
    for member in range(1, got_ref.shape[0]):
        total = total + got_ref[member].astype(jnp.float32)
    small = total[size : size + PART] + total[size + PART :]
    raw_gram, terms = unpack_small(small, size, trial_count)
    diagonal = raw_gram * eye_of(size)
    down = 1.0 / jnp.sqrt(jnp.sum(diagonal, axis=1, keepdims=True) / neuron_count + tiny_eps)
    across = 1.0 / jnp.sqrt(jnp.sum(diagonal, axis=0, keepdims=True) / neuron_count + tiny_eps)
    neuron_ref[...] = raw_ref[...] * down
    neuron_gram = down * raw_gram * across
    neuron_gram_ref[...] = neuron_gram
    trial_now = product(damped_inverse(neuron_gram * gram_ref[...]), terms * down)
    trial_ref[...] = trial_now
    trial_gram_ref[...] = gram_of(trial_now)
    lane = lax.broadcasted_iota(jnp.int32, trial_now.shape, 1)
    row = lax.broadcasted_iota(jnp.int32, (own_trials, trial_count), 0)
    column = lax.broadcasted_iota(jnp.int32, (own_trials, trial_count), 1)
    chosen = (column == plane * own_trials + row).astype(jnp.float32)
    own_ref[...] = rows_product(chosen, trial_now)
    columns = []
    for trial in range(own_trials):
        mine = lane == plane * own_trials + trial
        columns.append(jnp.sum(jnp.where(mine, trial_now, 0.0), axis=1, keepdims=True))
    lanes = total.shape[1]
    low = lax.broadcasted_iota(jnp.int32, (size, lanes), 1) < lanes // 2
    same = low == (lax.axis_index("pair") == 0)
    weighted = jnp.where(same, columns[0], columns[1]) * down * total[:size]
    weighted = weighted + pltpu.roll(weighted, lanes // 2, 1)
    half = size // 2
    weighted = jnp.where(low[:half], weighted[:half], weighted[half:])
    for member in range(sent_ref.shape[0]):
        sent_ref[member] = weighted


def sum_body(got_ref, sent_ref):
    total = got_ref[0]
    for member in range(1, got_ref.shape[0]):
        total = total + got_ref[member]
    for member in range(sent_ref.shape[0]):
        sent_ref[member] = total


def inverse_body(left_ref, right_ref, out_ref):
    out_ref[...] = damped_inverse(left_ref[...] * right_ref[...])


def time_of(got_ref, inverse_ref):
    members, half, lanes = got_ref.shape
    low = lax.broadcasted_iota(jnp.int32, (half, lanes), 1) < lanes // 2
    pieces = []
    for block in range(members // 2):
        one, two = got_ref[block], got_ref[members // 2 + block]
        upper = jnp.where(low, one, pltpu.roll(two, lanes // 2, 1))
        lower = jnp.where(low, pltpu.roll(one, lanes // 2, 1), two)
        pieces.append(jnp.concatenate([upper, lower], axis=0))
    raw = product(inverse_ref[...], jnp.concatenate(pieces, axis=1))
    mean = jnp.sum(raw * raw, axis=1, keepdims=True) / raw.shape[1]
    return raw, jnp.sqrt(mean + tiny_eps)


def next_body(got_ref, inverse_ref, tensor_ref, time_ref, sent_ref):
    raw, norm = time_of(got_ref, inverse_ref)
    time_now = raw / norm
    time_ref[...] = time_now
    put_projected(time_now, lambda trial: tensor_ref[trial], sent_ref)


def gram_body(time_ref, gram_ref):
    gram_ref[...] = gram_of(time_ref[...])


def next_inverse_body(time_ref, trial_gram_ref, gram_ref, inverse_ref):
    gram = gram_of(time_ref[...])
    gram_ref[...] = gram
    inverse_ref[...] = damped_inverse(gram * trial_gram_ref[...])


def last_body(got_ref, inverse_ref, time_ref):
    raw, norm = time_of(got_ref, inverse_ref)
    count, size = time_ref.shape
    lanes = got_ref.shape[2]
    position = lax.axis_index(("z", "pair", "y", "core", "x"))
    column = lax.broadcasted_iota(jnp.int32, raw.shape, 1)
    mine = jnp.where(column // count == position, raw, 0.0)
    picked = mine[:, :lanes]
    for start in range(lanes, raw.shape[1], lanes):
        picked = picked + mine[:, start : start + lanes]
    row = lax.broadcasted_iota(jnp.int32, (count, lanes), 0)
    lane = lax.broadcasted_iota(jnp.int32, (count, lanes), 1)
    chosen = (lane == position * count % lanes + row).astype(jnp.float32)
    time_ref[...] = rows_product(chosen, picked / norm)


def per_device(tensor, time_init, trial_init):
    own_trials, own_neurons, timepoints = tensor.shape
    components = time_init.shape[0]
    planes = lax.axis_size("x")
    short = ("y", "core")
    near = ("pair",) + short
    blocks, layers = lax.axis_size(short), lax.axis_size("z")
    twins = lax.axis_size("pair")
    neuron_count = own_neurons * blocks * twins * layers
    trial_count = own_trials * planes
    lanes = timepoints // blocks
    main = own_trials * components

    def shape(*dims, kind=jnp.float32):
        return jax.ShapeDtypeStruct(dims, kind)

    square = shape(components, components)
    neuron_outs = (
        shape(components, own_neurons),
        shape(twins * blocks, components + 2 * PART, lanes, kind=WIRE),
    )
    shared = project(
        shape(planes, main + PART, own_neurons), time_init, trial_init.T, tensor
    )
    shared = lax.all_to_all(shared, "x", 0, 0)
    time_gram = call(gram_body, square, time_init)
    raw, sent = call(first_neuron_body, neuron_outs, shared, time_gram, tensor)
    for sweep_index in range(SWEEPS):
        got = lax.all_to_all(sent, near, 0, 0)
        sent = call(reduce_body, shape(layers, components + 2 * PART, lanes, kind=WIRE), got)
        got = lax.all_to_all(sent, "z", 0, 0)
        neuron_now, neuron_gram, trial_now, trial_gram, own_trial, sent = call(
            lambda *refs: finish_body(neuron_count, *refs),
            (
                shape(components, own_neurons),
                square,
                shape(components, trial_count),
                square,
                shape(own_trials, components),
                shape(planes, components // 2, lanes),
            ),
            got,
            time_gram,
            raw,
            slow=(0, 4) if sweep_index == SWEEPS - 1 else (),
        )
        got = lax.all_to_all(sent, "x", 0, 0)
        sent = call(sum_body, shape(twins * blocks, components // 2, lanes), got)
        got = lax.all_to_all(sent, near, 0, 0)
        inverse = call(inverse_body, square, neuron_gram, trial_gram)
        if sweep_index == SWEEPS - 1:
            time_out = call(
                last_body,
                shape(timepoints // (layers * twins * blocks * planes), components),
                got,
                inverse,
                slow=(0,),
            )
            break
        time_now, shared = call(
            next_body,
            (shape(components, timepoints), shape(planes, main, own_neurons)),
            got,
            inverse,
            tensor,
        )
        shared = lax.all_to_all(shared, "x", 0, 0)
        time_gram, inverse = call(next_inverse_body, (square, square), time_now, trial_gram)
        raw, sent = call(neuron_body, neuron_outs, shared, trial_now, inverse, tensor)
    return (neuron_now, time_out.T, own_trial.T)


def solution(mesh):
    neuron, trial = mesh.shape["neuron"], mesh.shape["trial"]
    layers = neuron // 16
    fine = Mesh(
        mesh.devices.reshape(layers, 2, 4, 2, trial), ("z", "pair", "y", "core", "x")
    )
    rows = ("z", "pair", "y", "core")
    return jax.shard_map(
        per_device,
        mesh=fine,
        in_specs=(P("x", rows, None), P(), P(None, "x")),
        out_specs=(P(None, rows), P(None, rows + ("x",)), P(None, "x")),
        check_vma=False,
    )
```

```python
import jax
import jax.numpy as jnp
from jax import lax
from jax.experimental import pallas as pl
from jax.experimental.pallas import tpu as pltpu
from jax.sharding import Mesh, PartitionSpec as P

SWEEPS = 2


ridge_share = 0.1
tiny_eps = 1e-06
EXACT = lax.Precision.HIGHEST
PART = 8
WIRE = jnp.bfloat16


def gram_of(matrix):
    return lax.dot_general(
        matrix,
        matrix,
        (((1,), (1,)), ((), ())),
        precision=EXACT,
        preferred_element_type=jnp.float32,
    )


def product(left, right):
    return lax.dot_general(
        left,
        right,
        (((1,), (0,)), ((), ())),
        precision=EXACT,
        preferred_element_type=jnp.float32,
    )


def rows_product(left, right):
    return lax.dot_general(
        left,
        right,
        (((1,), (1,)), ((), ())),
        precision=EXACT,
        preferred_element_type=jnp.float32,
    )


def split(values):
    high = values.astype(WIRE).astype(jnp.float32)
    return jnp.concatenate([high, values - high], axis=0).astype(WIRE)


def eye_of(size):
    rows = lax.broadcasted_iota(jnp.int32, (size, size), 0)
    cols = lax.broadcasted_iota(jnp.int32, (size, size), 1)
    return (rows == cols).astype(jnp.float32)


def damped_inverse(system):
    size = system.shape[0]
    eye = eye_of(size)
    trace = jnp.sum(jnp.sum(system * eye, axis=1, keepdims=True), axis=0, keepdims=True)
    share = size / trace
    both = jnp.concatenate([system * share + ridge_share * eye, eye], axis=1)
    row = lax.broadcasted_iota(jnp.int32, both.shape, 0)

    def pivots(step):
        if step >= size:
            return []
        return [
            jnp.broadcast_to(both[:, place : place + 1], both.shape) for place in (step, step + 1)
        ]

    ahead = [pivots(0), pivots(2)]
    for step in range(0, size, 2):
        first, second = ahead[0]
        p00, p01 = first[step : step + 1], second[step : step + 1]
        p10, p11 = first[step + 1 : step + 2], second[step + 1 : step + 2]
        over = 1.0 / (p00 * p11 - p01 * p10)
        p00, p01, p10, p11 = p00 * over, p01 * over, p10 * over, p11 * over

        def cleared(matrix):
            upper, lower = matrix[step : step + 1], matrix[step + 1 : step + 2]
            new_upper = p11 * upper - p01 * lower
            new_lower = p00 * lower - p10 * upper
            rest = matrix - first * new_upper - second * new_lower
            return jnp.where(row == step, new_upper, jnp.where(row == step + 1, new_lower, rest))

        ahead = [[cleared(one) for one in ahead[1]], [cleared(one) for one in pivots(step + 4)]]
        both = cleared(both)
    return both[:, size:] * share


def pack_small(gram, terms):
    size = gram.shape[0]
    pieces = []
    for start in range(0, size, PART):
        pieces.append(gram[start : start + PART, start:])
    for start in range(0, size, PART):
        pieces.append(terms[start : start + PART])
    used = sum(piece.shape[1] for piece in pieces)
    pieces.append(jnp.zeros((PART, 128 - used), jnp.float32))
    return jnp.concatenate(pieces, axis=1)


def unpack_small(tile, size, count):
    rows, place = [], 0
    for start in range(0, size, PART):
        piece = tile[:, place : place + size - start]
        place += size - start
        if start:
            piece = jnp.concatenate([jnp.zeros((PART, start), jnp.float32), piece], axis=1)
        rows.append(piece)
    upper = jnp.concatenate(rows, axis=0)
    terms = []
    for start in range(0, size, PART):
        terms.append(tile[:, place : place + count])
        place += count
    row_part = lax.broadcasted_iota(jnp.int32, (size, size), 0) // PART
    col_part = lax.broadcasted_iota(jnp.int32, (size, size), 1) // PART
    return jnp.where(col_part >= row_part, upper, upper.T), jnp.concatenate(terms, axis=0)


def call(body, outs, *args, away=(), slow=()):
    single = not isinstance(outs, tuple)
    listed = (outs,) if single else outs
    args = [
        arg if place in away else pltpu.with_memory_space_constraint(arg, pltpu.VMEM)
        for place, arg in enumerate(args)
    ]
    shapes = tuple(
        out if place in slow else pltpu.VMEM(out.shape, out.dtype)
        for place, out in enumerate(listed)
    )
    result = pl.pallas_call(
        body,
        out_shape=shapes,
        in_specs=[pl.BlockSpec(memory_space=pltpu.VMEM) for _ in args],
        out_specs=tuple(pl.BlockSpec(memory_space=pltpu.VMEM) for _ in listed),
    )(*args)
    return result[0] if single else result


def put_projected(time_now, tensor_of, sent_ref):
    rounded = time_now.astype(jnp.bfloat16)
    size = time_now.shape[0]
    for trial in range(sent_ref.shape[1] // size):
        projected = lax.dot_general(
            rounded,
            tensor_of(trial),
            (((1,), (1,)), ((), ())),
            preferred_element_type=jnp.float32,
        )
        for member in range(sent_ref.shape[0]):
            sent_ref[member, trial * size : (trial + 1) * size, :] = projected


def project_body(time_hbm, trial_hbm, tensor_hbm, *refs):
    sent_ref, tensor_ref, gram_ref, time_ref, trial_ref, arrived = refs
    count, size = trial_ref.shape
    copies = [
        pltpu.make_async_copy(time_hbm, time_ref, arrived.at[0]),
        pltpu.make_async_copy(trial_hbm, trial_ref, arrived.at[1]),
    ]
    for trial in range(count):
        copies.append(
            pltpu.make_async_copy(tensor_hbm.at[trial], tensor_ref.at[trial], arrived.at[2 + trial])
        )
    for copy in copies:
        copy.start()
    copies[0].wait()
    gram_ref[...] = gram_of(time_ref[...])

    def tensor_of(trial):
        copies[2 + trial].wait()
        return tensor_ref[trial]

    put_projected(time_ref[...], tensor_of, sent_ref)
    copies[1].wait()
    lanes = sent_ref.shape[2]
    tile = jnp.concatenate([trial_ref[...], jnp.zeros((PART - count, size), jnp.float32)], axis=0)
    tile = jnp.concatenate([tile, jnp.zeros((PART, lanes - size), jnp.float32)], axis=1)
    for member in range(sent_ref.shape[0]):
        sent_ref[member, count * size :, :] = tile


def project(outs, time_init, trial_rows, tensor):
    return pl.pallas_call(
        project_body,
        out_shape=tuple(pltpu.VMEM(out.shape, out.dtype) for out in outs),
        in_specs=[pl.BlockSpec(memory_space=pl.ANY) for _ in range(3)],
        out_specs=tuple(pl.BlockSpec(memory_space=pltpu.VMEM) for _ in outs),
        scratch_shapes=[
            pltpu.VMEM(time_init.shape, time_init.dtype),
            pltpu.VMEM(trial_rows.shape, trial_rows.dtype),
            pltpu.SemaphoreType.DMA((2 + tensor.shape[0],)),
        ],
    )(time_init, trial_rows, tensor)


def put_neuron(trial_now, inverse, shared_ref, tensor_ref, raw_ref, sent_ref):
    size, trial_count = trial_now.shape
    own_trials = tensor_ref.shape[0]
    terms = []
    projected = []
    for trial in range(trial_count):
        start = trial % own_trials * size
        projected.append(shared_ref[trial // own_trials, start : start + size, :])
    neuron_terms = trial_now[:, 0:1] * projected[0]
    for trial in range(1, trial_count):
        neuron_terms = neuron_terms + trial_now[:, trial : trial + 1] * projected[trial]
    raw = product(inverse, neuron_terms)
    raw_ref[...] = raw
    lane = lax.broadcasted_iota(jnp.int32, (size, trial_count), 1)
    terms = jnp.zeros((size, trial_count), jnp.float32)
    for trial in range(trial_count):
        one = jnp.sum(raw * projected[trial], axis=1, keepdims=True)
        terms = jnp.where(lane == trial, one, terms)
    small = split(pack_small(gram_of(raw), terms))
    members, _, lanes = sent_ref.shape
    blocks = tensor_ref.shape[2] // lanes
    low = lax.broadcasted_iota(jnp.int32, (size, lanes), 1) < lanes // 2
    rounded = raw.astype(jnp.bfloat16)
    first = jnp.dot(rounded, tensor_ref[0], preferred_element_type=jnp.float32)
    second = jnp.dot(rounded, tensor_ref[1], preferred_element_type=jnp.float32)
    for block in range(blocks):
        start = block * lanes
        one = first[:, start : start + lanes]
        two = pltpu.roll(second[:, start : start + lanes], lanes // 2, 1)
        sent_ref[block, :size, :] = jnp.where(low, one, two).astype(WIRE)
        sent_ref[blocks + block, :size, :] = jnp.where(low, two, one).astype(WIRE)
    for member in range(members):
        sent_ref[member, size:, :] = small


def first_neuron_body(shared_ref, gram_ref, tensor_ref, raw_ref, sent_ref):
    own_trials = tensor_ref.shape[0]
    size = raw_ref.shape[0]
    main = own_trials * size
    lines = [
        shared_ref[member, main : main + own_trials, :size]
        for member in range(shared_ref.shape[0])
    ]
    trial_now = rows_product(eye_of(size), jnp.concatenate(lines, axis=0))
    inverse = damped_inverse(gram_of(trial_now) * gram_ref[...])
    put_neuron(trial_now, inverse, shared_ref, tensor_ref, raw_ref, sent_ref)


def neuron_body(shared_ref, trial_ref, inverse_ref, tensor_ref, raw_ref, sent_ref):
    put_neuron(trial_ref[...], inverse_ref[...], shared_ref, tensor_ref, raw_ref, sent_ref)


def reduce_body(got_ref, sent_ref):
    total = got_ref[0].astype(jnp.float32)
    for member in range(1, got_ref.shape[0]):
        total = total + got_ref[member].astype(jnp.float32)
    main = total.shape[0] - 2 * PART
    rounded = total[:main].astype(WIRE)
    halves = split(total[main : main + PART] + total[main + PART :])
    for member in range(sent_ref.shape[0]):
        sent_ref[member, :main, :] = rounded
        sent_ref[member, main:, :] = halves


def finish_body(neuron_count, own_trials, last, got_ref, gram_ref, raw_ref, *outs):
    neuron_gram_ref, trial_gram_ref, sent_ref, *rest = outs
    size = raw_ref.shape[0]
    trial_count = own_trials * sent_ref.shape[0]
    plane = lax.axis_index("x")
    total = got_ref[0].astype(jnp.float32)
    for member in range(1, got_ref.shape[0]):
        total = total + got_ref[member].astype(jnp.float32)
    small = total[size : size + PART] + total[size + PART :]
    raw_gram, terms = unpack_small(small, size, trial_count)
    diagonal = raw_gram * eye_of(size)
    down = 1.0 / jnp.sqrt(jnp.sum(diagonal, axis=1, keepdims=True) / neuron_count + tiny_eps)
    across = 1.0 / jnp.sqrt(jnp.sum(diagonal, axis=0, keepdims=True) / neuron_count + tiny_eps)
    neuron_gram = down * raw_gram * across
    neuron_gram_ref[...] = neuron_gram
    trial_now = product(damped_inverse(neuron_gram * gram_ref[...]), terms * down)
    trial_gram_ref[...] = gram_of(trial_now)
    lane = lax.broadcasted_iota(jnp.int32, trial_now.shape, 1)
    if last:
        neuron_ref, own_ref = rest
        neuron_ref[...] = raw_ref[...] * down
        row = lax.broadcasted_iota(jnp.int32, (own_trials, trial_count), 0)
        column = lax.broadcasted_iota(jnp.int32, (own_trials, trial_count), 1)
        chosen = (column == plane * own_trials + row).astype(jnp.float32)
        own_ref[...] = rows_product(chosen, trial_now)
    else:
        (trial_ref,) = rest
        trial_ref[...] = trial_now
    columns = []
    for trial in range(own_trials):
        mine = lane == plane * own_trials + trial
        columns.append(jnp.sum(jnp.where(mine, trial_now, 0.0), axis=1, keepdims=True))
    lanes = total.shape[1]
    low = lax.broadcasted_iota(jnp.int32, (size, lanes), 1) < lanes // 2
    same = low == (lax.axis_index("pair") == 0)
    weighted = jnp.where(same, columns[0], columns[1]) * down * total[:size]
    weighted = weighted + pltpu.roll(weighted, lanes // 2, 1)
    half = size // 2
    weighted = jnp.where(low[:half], weighted[:half], weighted[half:])
    for member in range(sent_ref.shape[0]):
        sent_ref[member] = weighted


def sum_body(got_ref, sent_ref):
    total = got_ref[0]
    for member in range(1, got_ref.shape[0]):
        total = total + got_ref[member]
    for member in range(sent_ref.shape[0]):
        sent_ref[member] = total


def time_of(got_ref, left_ref, right_ref):
    inverse = damped_inverse(left_ref[...] * right_ref[...])
    members, half, lanes = got_ref.shape
    low = lax.broadcasted_iota(jnp.int32, (half, lanes), 1) < lanes // 2
    pieces = []
    for block in range(members // 2):
        one, two = got_ref[block], got_ref[members // 2 + block]
        upper = jnp.where(low, one, pltpu.roll(two, lanes // 2, 1))
        lower = jnp.where(low, pltpu.roll(one, lanes // 2, 1), two)
        pieces.append(jnp.concatenate([upper, lower], axis=0))
    raw = product(inverse, jnp.concatenate(pieces, axis=1))
    mean = jnp.sum(raw * raw, axis=1, keepdims=True) / raw.shape[1]
    return raw, jnp.sqrt(mean + tiny_eps)


def next_body(got_ref, neuron_gram_ref, trial_gram_ref, tensor_ref, *outs):
    sent_ref, gram_ref, inverse_ref = outs
    raw, norm = time_of(got_ref, neuron_gram_ref, trial_gram_ref)
    time_now = raw / norm
    put_projected(time_now, lambda trial: tensor_ref[trial], sent_ref)
    gram = gram_of(time_now)
    gram_ref[...] = gram
    inverse_ref[...] = damped_inverse(gram * trial_gram_ref[...])


def last_body(got_ref, neuron_gram_ref, trial_gram_ref, *refs):
    held_neuron_ref, held_own_ref, neuron_ref, time_ref, own_ref = refs
    neuron_ref[...] = held_neuron_ref[...]
    own_ref[...] = held_own_ref[...]
    raw, norm = time_of(got_ref, neuron_gram_ref, trial_gram_ref)
    count, size = time_ref.shape
    lanes = got_ref.shape[2]
    position = lax.axis_index(("z", "pair", "y", "core", "x"))
    column = lax.broadcasted_iota(jnp.int32, raw.shape, 1)
    mine = jnp.where(column // count == position, raw, 0.0)
    picked = mine[:, :lanes]
    for start in range(lanes, raw.shape[1], lanes):
        picked = picked + mine[:, start : start + lanes]
    row = lax.broadcasted_iota(jnp.int32, (count, lanes), 0)
    lane = lax.broadcasted_iota(jnp.int32, (count, lanes), 1)
    chosen = (lane == position * count % lanes + row).astype(jnp.float32)
    time_ref[...] = rows_product(chosen, picked / norm)


def per_device(tensor, time_init, trial_init):
    own_trials, own_neurons, timepoints = tensor.shape
    components = time_init.shape[0]
    planes = lax.axis_size("x")
    short = ("y", "core")
    near = ("pair",) + short
    blocks, layers = lax.axis_size(short), lax.axis_size("z")
    twins = lax.axis_size("pair")
    neuron_count = own_neurons * blocks * twins * layers
    trial_count = own_trials * planes
    lanes = timepoints // blocks
    main = own_trials * components

    def shape(*dims, kind=jnp.float32):
        return jax.ShapeDtypeStruct(dims, kind)

    square = shape(components, components)
    neuron_outs = (
        shape(components, own_neurons),
        shape(twins * blocks, components + 2 * PART, lanes, kind=WIRE),
    )
    shared, tensor, time_gram = project(
        (
            shape(planes, main + PART, own_neurons),
            shape(own_trials, own_neurons, timepoints, kind=tensor.dtype),
            square,
        ),
        time_init,
        trial_init.T,
        tensor,
    )
    shared = lax.all_to_all(shared, "x", 0, 0)
    raw, sent = call(first_neuron_body, neuron_outs, shared, time_gram, tensor)
    for sweep_index in range(SWEEPS):
        got = lax.all_to_all(sent, near, 0, 0)
        sent = call(reduce_body, shape(layers, components + 2 * PART, lanes, kind=WIRE), got)
        got = lax.all_to_all(sent, "z", 0, 0)
        last = sweep_index == SWEEPS - 1
        neuron_shape = shape(components, own_neurons)
        own_shape = shape(own_trials, components)
        extra = (neuron_shape, own_shape) if last else (shape(components, trial_count),)
        neuron_gram, trial_gram, sent, *rest = call(
            lambda *refs: finish_body(neuron_count, own_trials, last, *refs),
            (square, square, shape(planes, components // 2, lanes)) + extra,
            got,
            time_gram,
            raw,
        )
        got = lax.all_to_all(sent, "x", 0, 0)
        sent = call(sum_body, shape(twins * blocks, components // 2, lanes), got)
        got = lax.all_to_all(sent, near, 0, 0)
        if last:
            share_width = timepoints // (layers * twins * blocks * planes)
            neuron_now, time_out, own_trial = call(
                last_body,
                (neuron_shape, shape(share_width, components), own_shape),
                got,
                neuron_gram,
                trial_gram,
                *rest,
                slow=(0, 1, 2),
            )
            break
        shared, time_gram, inverse = call(
            next_body,
            (shape(planes, main, own_neurons), square, square),
            got,
            neuron_gram,
            trial_gram,
            tensor,
        )
        shared = lax.all_to_all(shared, "x", 0, 0)
        raw, sent = call(neuron_body, neuron_outs, shared, rest[0], inverse, tensor)
    return (neuron_now, time_out.T, own_trial.T)


def solution(mesh):
    neuron, trial = mesh.shape["neuron"], mesh.shape["trial"]
    layers = neuron // 16
    fine = Mesh(
        mesh.devices.reshape(layers, 2, 4, 2, trial), ("z", "pair", "y", "core", "x")
    )
    rows = ("z", "pair", "y", "core")
    return jax.shard_map(
        per_device,
        mesh=fine,
        in_specs=(P("x", rows, None), P(), P(None, "x")),
        out_specs=(P(None, rows), P(None, rows + ("x",)), P(None, "x")),
        check_vma=False,
    )
```

```python
import jax
import jax.numpy as jnp
from jax import lax
from jax.experimental import pallas as pl
from jax.experimental.pallas import tpu as pltpu
from jax.sharding import Mesh, PartitionSpec as P

SWEEPS = 2


ridge_share = 0.1
tiny_eps = 1e-06
EXACT = lax.Precision.HIGHEST
PART = 8
AHEAD = 3
WIRE = jnp.bfloat16


def gram_of(matrix):
    return lax.dot_general(
        matrix,
        matrix,
        (((1,), (1,)), ((), ())),
        precision=EXACT,
        preferred_element_type=jnp.float32,
    )


def product(left, right):
    return lax.dot_general(
        left,
        right,
        (((1,), (0,)), ((), ())),
        precision=EXACT,
        preferred_element_type=jnp.float32,
    )


def rows_product(left, right):
    return lax.dot_general(
        left,
        right,
        (((1,), (1,)), ((), ())),
        precision=EXACT,
        preferred_element_type=jnp.float32,
    )


def split(values):
    high = values.astype(WIRE).astype(jnp.float32)
    return jnp.concatenate([high, values - high], axis=0).astype(WIRE)


def eye_of(size):
    rows = lax.broadcasted_iota(jnp.int32, (size, size), 0)
    cols = lax.broadcasted_iota(jnp.int32, (size, size), 1)
    return (rows == cols).astype(jnp.float32)


def damped_inverse(system):
    size = system.shape[0]
    eye = eye_of(size)
    trace = jnp.sum(jnp.sum(system * eye, axis=1, keepdims=True), axis=0, keepdims=True)
    share = size / trace
    both = system * share + ridge_share * eye
    row = lax.broadcasted_iota(jnp.int32, both.shape, 0)
    lane = lax.broadcasted_iota(jnp.int32, both.shape, 1)

    def pivots(step):
        if step >= size:
            return []
        return [
            jnp.broadcast_to(both[:, place : place + 1], both.shape) for place in (step, step + 1)
        ]

    ahead = [pivots(2 * place) for place in range(AHEAD)]
    for step in range(0, size, 2):
        first, second = ahead[0]
        p00, p01 = first[step : step + 1], second[step : step + 1]
        p10, p11 = first[step + 1 : step + 2], second[step + 1 : step + 2]
        over = 1.0 / (p00 * p11 - p01 * p10)
        p00, p01, p10, p11 = p00 * over, p01 * over, p10 * over, p11 * over

        def cleared(matrix):
            upper, lower = matrix[step : step + 1], matrix[step + 1 : step + 2]
            new_upper = p11 * upper - p01 * lower
            new_lower = p00 * lower - p10 * upper
            rest = matrix - first * new_upper - second * new_lower
            return jnp.where(row == step, new_upper, jnp.where(row == step + 1, new_lower, rest))

        ahead = [[cleared(one) for one in pair] for pair in ahead[1:] + [pivots(step + 2 * AHEAD)]]
        inner = jnp.logical_or(lane == step, lane == step + 1)
        both = cleared(jnp.where(inner, eye, both))
    return both * share


def pack_small(gram, terms):
    size = gram.shape[0]
    pieces = []
    for start in range(0, size, PART):
        pieces.append(gram[start : start + PART, start:])
    for start in range(0, size, PART):
        pieces.append(terms[start : start + PART])
    used = sum(piece.shape[1] for piece in pieces)
    pieces.append(jnp.zeros((PART, 128 - used), jnp.float32))
    return jnp.concatenate(pieces, axis=1)


def unpack_small(tile, size, count):
    rows, place = [], 0
    for start in range(0, size, PART):
        piece = tile[:, place : place + size - start]
        place += size - start
        if start:
            piece = jnp.concatenate([jnp.zeros((PART, start), jnp.float32), piece], axis=1)
        rows.append(piece)
    upper = jnp.concatenate(rows, axis=0)
    terms = []
    for start in range(0, size, PART):
        terms.append(tile[:, place : place + count])
        place += count
    row_part = lax.broadcasted_iota(jnp.int32, (size, size), 0) // PART
    col_part = lax.broadcasted_iota(jnp.int32, (size, size), 1) // PART
    return jnp.where(col_part >= row_part, upper, upper.T), jnp.concatenate(terms, axis=0)


def call(body, outs, *args, away=(), slow=()):
    single = not isinstance(outs, tuple)
    listed = (outs,) if single else outs
    args = [
        arg if place in away else pltpu.with_memory_space_constraint(arg, pltpu.VMEM)
        for place, arg in enumerate(args)
    ]
    shapes = tuple(
        out if place in slow else pltpu.VMEM(out.shape, out.dtype)
        for place, out in enumerate(listed)
    )
    result = pl.pallas_call(
        body,
        out_shape=shapes,
        in_specs=[pl.BlockSpec(memory_space=pltpu.VMEM) for _ in args],
        out_specs=tuple(pl.BlockSpec(memory_space=pltpu.VMEM) for _ in listed),
    )(*args)
    return result[0] if single else result


def put_projected(time_now, tensor_of, sent_ref):
    rounded = time_now.astype(jnp.bfloat16)
    size = time_now.shape[0]
    for trial in range(sent_ref.shape[1] // size):
        projected = lax.dot_general(
            rounded,
            tensor_of(trial),
            (((1,), (1,)), ((), ())),
            preferred_element_type=jnp.float32,
        )
        for member in range(sent_ref.shape[0]):
            sent_ref[member, trial * size : (trial + 1) * size, :] = projected


def project_body(time_hbm, trial_hbm, tensor_hbm, *refs):
    sent_ref, tensor_ref, gram_ref, time_ref, trial_ref, arrived = refs
    count, size = trial_ref.shape
    copies = [
        pltpu.make_async_copy(time_hbm, time_ref, arrived.at[0]),
        pltpu.make_async_copy(trial_hbm, trial_ref, arrived.at[1]),
    ]
    for trial in range(count):
        copies.append(
            pltpu.make_async_copy(tensor_hbm.at[trial], tensor_ref.at[trial], arrived.at[2 + trial])
        )
    for copy in copies:
        copy.start()
    copies[0].wait()
    gram_ref[...] = gram_of(time_ref[...])

    def tensor_of(trial):
        copies[2 + trial].wait()
        return tensor_ref[trial]

    put_projected(time_ref[...], tensor_of, sent_ref)
    copies[1].wait()
    lanes = sent_ref.shape[2]
    tile = jnp.concatenate([trial_ref[...], jnp.zeros((PART - count, size), jnp.float32)], axis=0)
    tile = jnp.concatenate([tile, jnp.zeros((PART, lanes - size), jnp.float32)], axis=1)
    for member in range(sent_ref.shape[0]):
        sent_ref[member, count * size :, :] = tile


def project(outs, time_init, trial_rows, tensor):
    return pl.pallas_call(
        project_body,
        out_shape=tuple(pltpu.VMEM(out.shape, out.dtype) for out in outs),
        in_specs=[pl.BlockSpec(memory_space=pl.ANY) for _ in range(3)],
        out_specs=tuple(pl.BlockSpec(memory_space=pltpu.VMEM) for _ in outs),
        scratch_shapes=[
            pltpu.VMEM(time_init.shape, time_init.dtype),
            pltpu.VMEM(trial_rows.shape, trial_rows.dtype),
            pltpu.SemaphoreType.DMA((2 + tensor.shape[0],)),
        ],
    )(time_init, trial_rows, tensor)


def put_neuron(trial_now, inverse, shared_ref, tensor_ref, raw_ref, sent_ref):
    size, trial_count = trial_now.shape
    own_trials = tensor_ref.shape[0]
    terms = []
    projected = []
    for trial in range(trial_count):
        start = trial % own_trials * size
        projected.append(shared_ref[trial // own_trials, start : start + size, :])
    neuron_terms = trial_now[:, 0:1] * projected[0]
    for trial in range(1, trial_count):
        neuron_terms = neuron_terms + trial_now[:, trial : trial + 1] * projected[trial]
    raw = product(inverse, neuron_terms)
    raw_ref[...] = raw
    lane = lax.broadcasted_iota(jnp.int32, (size, trial_count), 1)
    terms = jnp.zeros((size, trial_count), jnp.float32)
    for trial in range(trial_count):
        one = jnp.sum(raw * projected[trial], axis=1, keepdims=True)
        terms = jnp.where(lane == trial, one, terms)
    small = split(pack_small(gram_of(raw), terms))
    members, _, lanes = sent_ref.shape
    blocks = tensor_ref.shape[2] // lanes
    low = lax.broadcasted_iota(jnp.int32, (size, lanes), 1) < lanes // 2
    rounded = raw.astype(jnp.bfloat16)
    first = jnp.dot(rounded, tensor_ref[0], preferred_element_type=jnp.float32)
    second = jnp.dot(rounded, tensor_ref[1], preferred_element_type=jnp.float32)
    for block in range(blocks):
        start = block * lanes
        one = first[:, start : start + lanes]
        two = pltpu.roll(second[:, start : start + lanes], lanes // 2, 1)
        sent_ref[block, :size, :] = jnp.where(low, one, two).astype(WIRE)
        sent_ref[blocks + block, :size, :] = jnp.where(low, two, one).astype(WIRE)
    for member in range(members):
        sent_ref[member, size:, :] = small


def first_neuron_body(shared_ref, gram_ref, tensor_ref, raw_ref, sent_ref):
    own_trials = tensor_ref.shape[0]
    size = raw_ref.shape[0]
    main = own_trials * size
    lines = [
        shared_ref[member, main : main + own_trials, :size]
        for member in range(shared_ref.shape[0])
    ]
    trial_now = rows_product(eye_of(size), jnp.concatenate(lines, axis=0))
    inverse = damped_inverse(gram_of(trial_now) * gram_ref[...])
    put_neuron(trial_now, inverse, shared_ref, tensor_ref, raw_ref, sent_ref)


def neuron_body(shared_ref, trial_ref, inverse_ref, tensor_ref, raw_ref, sent_ref):
    put_neuron(trial_ref[...], inverse_ref[...], shared_ref, tensor_ref, raw_ref, sent_ref)


def reduce_body(got_ref, sent_ref):
    total = got_ref[0].astype(jnp.float32)
    for member in range(1, got_ref.shape[0]):
        total = total + got_ref[member].astype(jnp.float32)
    main = total.shape[0] - 2 * PART
    rounded = total[:main].astype(WIRE)
    halves = split(total[main : main + PART] + total[main + PART :])
    for member in range(sent_ref.shape[0]):
        sent_ref[member, :main, :] = rounded
        sent_ref[member, main:, :] = halves


def finish_body(neuron_count, own_trials, last, got_ref, gram_ref, raw_ref, *outs):
    neuron_gram_ref, trial_gram_ref, sent_ref, *rest = outs
    size = raw_ref.shape[0]
    trial_count = own_trials * sent_ref.shape[0]
    plane = lax.axis_index("x")
    total = got_ref[0].astype(jnp.float32)
    for member in range(1, got_ref.shape[0]):
        total = total + got_ref[member].astype(jnp.float32)
    small = total[size : size + PART] + total[size + PART :]
    raw_gram, terms = unpack_small(small, size, trial_count)
    diagonal = raw_gram * eye_of(size)
    down = 1.0 / jnp.sqrt(jnp.sum(diagonal, axis=1, keepdims=True) / neuron_count + tiny_eps)
    across = 1.0 / jnp.sqrt(jnp.sum(diagonal, axis=0, keepdims=True) / neuron_count + tiny_eps)
    neuron_gram = down * raw_gram * across
    neuron_gram_ref[...] = neuron_gram
    trial_now = product(damped_inverse(neuron_gram * gram_ref[...]), terms * down)
    trial_gram_ref[...] = gram_of(trial_now)
    lane = lax.broadcasted_iota(jnp.int32, trial_now.shape, 1)
    if last:
        neuron_ref, own_ref = rest
        neuron_ref[...] = raw_ref[...] * down
        row = lax.broadcasted_iota(jnp.int32, (own_trials, trial_count), 0)
        column = lax.broadcasted_iota(jnp.int32, (own_trials, trial_count), 1)
        chosen = (column == plane * own_trials + row).astype(jnp.float32)
        own_ref[...] = rows_product(chosen, trial_now)
    else:
        (trial_ref,) = rest
        trial_ref[...] = trial_now
    columns = []
    for trial in range(own_trials):
        mine = lane == plane * own_trials + trial
        columns.append(jnp.sum(jnp.where(mine, trial_now, 0.0), axis=1, keepdims=True))
    lanes = total.shape[1]
    low = lax.broadcasted_iota(jnp.int32, (size, lanes), 1) < lanes // 2
    same = low == (lax.axis_index("pair") == 0)
    weighted = jnp.where(same, columns[0], columns[1]) * down * total[:size]
    weighted = weighted + pltpu.roll(weighted, lanes // 2, 1)
    half = size // 2
    weighted = jnp.where(low[:half], weighted[:half], weighted[half:])
    for member in range(sent_ref.shape[0]):
        sent_ref[member] = weighted


def sum_body(got_ref, sent_ref):
    total = got_ref[0]
    for member in range(1, got_ref.shape[0]):
        total = total + got_ref[member]
    for member in range(sent_ref.shape[0]):
        sent_ref[member] = total


def time_of(got_ref, left_ref, right_ref):
    inverse = damped_inverse(left_ref[...] * right_ref[...])
    members, half, lanes = got_ref.shape
    low = lax.broadcasted_iota(jnp.int32, (half, lanes), 1) < lanes // 2
    pieces = []
    for block in range(members // 2):
        one, two = got_ref[block], got_ref[members // 2 + block]
        upper = jnp.where(low, one, pltpu.roll(two, lanes // 2, 1))
        lower = jnp.where(low, pltpu.roll(one, lanes // 2, 1), two)
        pieces.append(jnp.concatenate([upper, lower], axis=0))
    return product(inverse, jnp.concatenate(pieces, axis=1))


def next_body(got_ref, neuron_gram_ref, trial_gram_ref, tensor_ref, *outs):
    sent_ref, gram_ref, inverse_ref = outs
    raw = time_of(got_ref, neuron_gram_ref, trial_gram_ref)
    raw_gram = gram_of(raw)
    diagonal = raw_gram * eye_of(raw.shape[0])
    count = raw.shape[1]
    down = 1.0 / jnp.sqrt(jnp.sum(diagonal, axis=1, keepdims=True) / count + tiny_eps)
    across = 1.0 / jnp.sqrt(jnp.sum(diagonal, axis=0, keepdims=True) / count + tiny_eps)
    put_projected(raw * down, lambda trial: tensor_ref[trial], sent_ref)
    gram = down * raw_gram * across
    gram_ref[...] = gram
    inverse_ref[...] = damped_inverse(gram * trial_gram_ref[...])


def last_body(got_ref, neuron_gram_ref, trial_gram_ref, *refs):
    held_neuron_ref, held_own_ref, neuron_ref, time_ref, own_ref = refs
    neuron_ref[...] = held_neuron_ref[...]
    own_ref[...] = held_own_ref[...]
    raw = time_of(got_ref, neuron_gram_ref, trial_gram_ref)
    mean = jnp.sum(raw * raw, axis=1, keepdims=True) / raw.shape[1]
    down = 1.0 / jnp.sqrt(mean + tiny_eps)
    count, size = time_ref.shape
    lanes = got_ref.shape[2]
    position = lax.axis_index(("z", "pair", "y", "core", "x"))
    column = lax.broadcasted_iota(jnp.int32, raw.shape, 1)
    mine = jnp.where(column // count == position, raw, 0.0)
    picked = mine[:, :lanes]
    for start in range(lanes, raw.shape[1], lanes):
        picked = picked + mine[:, start : start + lanes]
    row = lax.broadcasted_iota(jnp.int32, (count, lanes), 0)
    lane = lax.broadcasted_iota(jnp.int32, (count, lanes), 1)
    chosen = (lane == position * count % lanes + row).astype(jnp.float32)
    time_ref[...] = rows_product(chosen, picked * down)


def per_device(tensor, time_init, trial_init):
    own_trials, own_neurons, timepoints = tensor.shape
    components = time_init.shape[0]
    planes = lax.axis_size("x")
    short = ("y", "core")
    near = ("pair",) + short
    blocks, layers = lax.axis_size(short), lax.axis_size("z")
    twins = lax.axis_size("pair")
    neuron_count = own_neurons * blocks * twins * layers
    trial_count = own_trials * planes
    lanes = timepoints // blocks
    main = own_trials * components

    def shape(*dims, kind=jnp.float32):
        return jax.ShapeDtypeStruct(dims, kind)

    square = shape(components, components)
    neuron_outs = (
        shape(components, own_neurons),
        shape(twins * blocks, components + 2 * PART, lanes, kind=WIRE),
    )
    shared, tensor, time_gram = project(
        (
            shape(planes, main + PART, own_neurons),
            shape(own_trials, own_neurons, timepoints, kind=tensor.dtype),
            square,
        ),
        time_init,
        trial_init.T,
        tensor,
    )
    shared = lax.all_to_all(shared, "x", 0, 0)
    raw, sent = call(first_neuron_body, neuron_outs, shared, time_gram, tensor)
    for sweep_index in range(SWEEPS):
        got = lax.all_to_all(sent, near, 0, 0)
        sent = call(reduce_body, shape(layers, components + 2 * PART, lanes, kind=WIRE), got)
        got = lax.all_to_all(sent, "z", 0, 0)
        last = sweep_index == SWEEPS - 1
        neuron_shape = shape(components, own_neurons)
        own_shape = shape(own_trials, components)
        extra = (neuron_shape, own_shape) if last else (shape(components, trial_count),)
        neuron_gram, trial_gram, sent, *rest = call(
            lambda *refs: finish_body(neuron_count, own_trials, last, *refs),
            (square, square, shape(planes, components // 2, lanes)) + extra,
            got,
            time_gram,
            raw,
        )
        got = lax.all_to_all(sent, "x", 0, 0)
        sent = call(sum_body, shape(twins * blocks, components // 2, lanes), got)
        got = lax.all_to_all(sent, near, 0, 0)
        if last:
            share_width = timepoints // (layers * twins * blocks * planes)
            neuron_now, time_out, own_trial = call(
                last_body,
                (neuron_shape, shape(share_width, components), own_shape),
                got,
                neuron_gram,
                trial_gram,
                *rest,
                slow=(0, 1, 2),
            )
            break
        shared, time_gram, inverse = call(
            next_body,
            (shape(planes, main, own_neurons), square, square),
            got,
            neuron_gram,
            trial_gram,
            tensor,
        )
        shared = lax.all_to_all(shared, "x", 0, 0)
        raw, sent = call(neuron_body, neuron_outs, shared, rest[0], inverse, tensor)
    return (neuron_now, time_out.T, own_trial.T)


def solution(mesh):
    neuron, trial = mesh.shape["neuron"], mesh.shape["trial"]
    layers = neuron // 16
    fine = Mesh(
        mesh.devices.reshape(layers, 2, 4, 2, trial), ("z", "pair", "y", "core", "x")
    )
    rows = ("z", "pair", "y", "core")
    return jax.shard_map(
        per_device,
        mesh=fine,
        in_specs=(P("x", rows, None), P(), P(None, "x")),
        out_specs=(P(None, rows), P(None, rows + ("x",)), P(None, "x")),
        check_vma=False,
    )
```

```python
import jax
import jax.numpy as jnp
from jax import lax
from jax.experimental import pallas as pl
from jax.experimental.pallas import tpu as pltpu
from jax.sharding import Mesh, PartitionSpec as P

SWEEPS = 2


ridge_share = 0.1
tiny_eps = 1e-06
EXACT = lax.Precision.HIGHEST
PART = 8
AHEAD = 3
WIRE = jnp.bfloat16


def gram_of(matrix):
    return lax.dot_general(
        matrix,
        matrix,
        (((1,), (1,)), ((), ())),
        precision=EXACT,
        preferred_element_type=jnp.float32,
    )


def product(left, right):
    return lax.dot_general(
        left,
        right,
        (((1,), (0,)), ((), ())),
        precision=EXACT,
        preferred_element_type=jnp.float32,
    )


def rows_product(left, right):
    return lax.dot_general(
        left,
        right,
        (((1,), (1,)), ((), ())),
        precision=EXACT,
        preferred_element_type=jnp.float32,
    )


def split(values):
    high = values.astype(WIRE).astype(jnp.float32)
    return jnp.concatenate([high, values - high], axis=0).astype(WIRE)


def eye_of(size):
    rows = lax.broadcasted_iota(jnp.int32, (size, size), 0)
    cols = lax.broadcasted_iota(jnp.int32, (size, size), 1)
    return (rows == cols).astype(jnp.float32)


def damped_inverse(system):
    size = system.shape[0]
    eye = eye_of(size)
    trace = jnp.sum(jnp.sum(system * eye, axis=1, keepdims=True), axis=0, keepdims=True)
    share = size / trace
    both = system * share + ridge_share * eye
    row = lax.broadcasted_iota(jnp.int32, both.shape, 0)
    lane = lax.broadcasted_iota(jnp.int32, both.shape, 1)

    def pivots(step):
        if step >= size:
            return []
        return [
            jnp.broadcast_to(both[:, place : place + 1], both.shape) for place in (step, step + 1)
        ]

    ahead = [pivots(2 * place) for place in range(AHEAD)]
    for step in range(0, size, 2):
        first, second = ahead[0]
        p00, p01 = first[step : step + 1], second[step : step + 1]
        p10, p11 = first[step + 1 : step + 2], second[step + 1 : step + 2]
        over = 1.0 / (p00 * p11 - p01 * p10)
        p00, p01, p10, p11 = p00 * over, p01 * over, p10 * over, p11 * over

        def cleared(matrix):
            upper, lower = matrix[step : step + 1], matrix[step + 1 : step + 2]
            new_upper = p11 * upper - p01 * lower
            new_lower = p00 * lower - p10 * upper
            rest = matrix - first * new_upper - second * new_lower
            return jnp.where(row == step, new_upper, jnp.where(row == step + 1, new_lower, rest))

        ahead = [[cleared(one) for one in pair] for pair in ahead[1:] + [pivots(step + 2 * AHEAD)]]
        inner = jnp.logical_or(lane == step, lane == step + 1)
        both = cleared(jnp.where(inner, eye, both))
    return both * share


def pack_small(gram, terms):
    size = gram.shape[0]
    pieces = []
    for start in range(0, size, PART):
        pieces.append(gram[start : start + PART, start:])
    for start in range(0, size, PART):
        pieces.append(terms[start : start + PART])
    used = sum(piece.shape[1] for piece in pieces)
    pieces.append(jnp.zeros((PART, 128 - used), jnp.float32))
    return jnp.concatenate(pieces, axis=1)


def unpack_small(tile, size, count):
    rows, place = [], 0
    for start in range(0, size, PART):
        piece = tile[:, place : place + size - start]
        place += size - start
        if start:
            piece = jnp.concatenate([jnp.zeros((PART, start), jnp.float32), piece], axis=1)
        rows.append(piece)
    upper = jnp.concatenate(rows, axis=0)
    terms = []
    for start in range(0, size, PART):
        terms.append(tile[:, place : place + count])
        place += count
    row_part = lax.broadcasted_iota(jnp.int32, (size, size), 0) // PART
    col_part = lax.broadcasted_iota(jnp.int32, (size, size), 1) // PART
    return jnp.where(col_part >= row_part, upper, upper.T), jnp.concatenate(terms, axis=0)


def call(body, outs, *args, away=(), slow=()):
    single = not isinstance(outs, tuple)
    listed = (outs,) if single else outs
    args = [
        arg if place in away else pltpu.with_memory_space_constraint(arg, pltpu.VMEM)
        for place, arg in enumerate(args)
    ]
    shapes = tuple(
        out if place in slow else pltpu.VMEM(out.shape, out.dtype)
        for place, out in enumerate(listed)
    )
    result = pl.pallas_call(
        body,
        out_shape=shapes,
        in_specs=[pl.BlockSpec(memory_space=pltpu.VMEM) for _ in args],
        out_specs=tuple(pl.BlockSpec(memory_space=pltpu.VMEM) for _ in listed),
    )(*args)
    return result[0] if single else result


def put_projected(time_now, trial_own, tensor_of, projected_ref, sent_ref):
    rounded = time_now.astype(jnp.bfloat16)
    size = time_now.shape[0]
    part = None
    for trial in range(trial_own.shape[1]):
        projected = lax.dot_general(
            rounded,
            tensor_of(trial),
            (((1,), (1,)), ((), ())),
            preferred_element_type=jnp.float32,
        )
        projected_ref[trial] = projected
        scaled = trial_own[:, trial : trial + 1] * projected
        part = scaled if part is None else part + scaled
    for member in range(sent_ref.shape[0]):
        sent_ref[member, :size, :] = part


def tile_of(rows, lanes):
    count, size = rows.shape
    tile = jnp.concatenate([rows, jnp.zeros((PART - count, size), jnp.float32)], axis=0)
    return jnp.concatenate([tile, jnp.zeros((PART, lanes - size), jnp.float32)], axis=1)


def trial_of(got_ref, start, count, size):
    lines = [got_ref[member, start : start + count, :size] for member in range(got_ref.shape[0])]
    return rows_product(eye_of(size), jnp.concatenate(lines, axis=0))


def project_body(time_hbm, trial_hbm, tensor_hbm, *refs):
    sent_ref, projected_ref, tensor_ref, gram_ref, time_ref, trial_ref, arrived = refs
    count, size = trial_ref.shape
    copies = [
        pltpu.make_async_copy(time_hbm, time_ref, arrived.at[0]),
        pltpu.make_async_copy(trial_hbm, trial_ref, arrived.at[1]),
    ]
    for trial in range(count):
        copies.append(
            pltpu.make_async_copy(tensor_hbm.at[trial], tensor_ref.at[trial], arrived.at[2 + trial])
        )
    for copy in copies:
        copy.start()
    copies[0].wait()
    gram_ref[...] = gram_of(time_ref[...])

    def tensor_of(trial):
        copies[2 + trial].wait()
        return tensor_ref[trial]

    copies[1].wait()
    trial_own = rows_product(eye_of(size), trial_ref[...])
    put_projected(time_ref[...], trial_own, tensor_of, projected_ref, sent_ref)
    tile = tile_of(trial_ref[...], sent_ref.shape[2])
    for member in range(sent_ref.shape[0]):
        sent_ref[member, size:, :] = tile


def project(outs, time_init, trial_rows, tensor):
    return pl.pallas_call(
        project_body,
        out_shape=tuple(pltpu.VMEM(out.shape, out.dtype) for out in outs),
        in_specs=[pl.BlockSpec(memory_space=pl.ANY) for _ in range(3)],
        out_specs=tuple(pl.BlockSpec(memory_space=pltpu.VMEM) for _ in outs),
        scratch_shapes=[
            pltpu.VMEM(time_init.shape, time_init.dtype),
            pltpu.VMEM(trial_rows.shape, trial_rows.dtype),
            pltpu.SemaphoreType.DMA((2 + tensor.shape[0],)),
        ],
    )(time_init, trial_rows, tensor)


def put_neuron(inverse, shared_ref, projected_ref, tensor_ref, raw_ref, sent_ref):
    own_trials, size, _ = projected_ref.shape
    neuron_terms = shared_ref[0, :size, :]
    for member in range(1, shared_ref.shape[0]):
        neuron_terms = neuron_terms + shared_ref[member, :size, :]
    raw = product(inverse, neuron_terms)
    raw_ref[...] = raw
    terms = [
        jnp.sum(raw * projected_ref[trial], axis=1, keepdims=True) for trial in range(own_trials)
    ]
    terms = jnp.concatenate(terms, axis=1)
    small = split(pack_small(gram_of(raw), terms))
    members, _, lanes = sent_ref.shape
    blocks = tensor_ref.shape[2] // lanes
    low = lax.broadcasted_iota(jnp.int32, (size, lanes), 1) < lanes // 2
    rounded = raw.astype(jnp.bfloat16)
    first = jnp.dot(rounded, tensor_ref[0], preferred_element_type=jnp.float32)
    second = jnp.dot(rounded, tensor_ref[1], preferred_element_type=jnp.float32)
    for block in range(blocks):
        start = block * lanes
        one = first[:, start : start + lanes]
        two = pltpu.roll(second[:, start : start + lanes], lanes // 2, 1)
        sent_ref[block, :size, :] = jnp.where(low, one, two).astype(WIRE)
        sent_ref[blocks + block, :size, :] = jnp.where(low, two, one).astype(WIRE)
    for member in range(members):
        sent_ref[member, size:, :] = small


def first_neuron_body(shared_ref, projected_ref, gram_ref, tensor_ref, raw_ref, sent_ref):
    own_trials, size, _ = projected_ref.shape
    trial_now = trial_of(shared_ref, size, own_trials, size)
    inverse = damped_inverse(gram_of(trial_now) * gram_ref[...])
    put_neuron(inverse, shared_ref, projected_ref, tensor_ref, raw_ref, sent_ref)


def neuron_body(shared_ref, projected_ref, inverse_ref, tensor_ref, raw_ref, sent_ref):
    put_neuron(inverse_ref[...], shared_ref, projected_ref, tensor_ref, raw_ref, sent_ref)


def reduce_body(got_ref, sent_ref):
    total = got_ref[0].astype(jnp.float32)
    for member in range(1, got_ref.shape[0]):
        total = total + got_ref[member].astype(jnp.float32)
    main = total.shape[0] - 2 * PART
    rounded = total[:main].astype(WIRE)
    halves = split(total[main : main + PART] + total[main + PART :])
    for member in range(sent_ref.shape[0]):
        sent_ref[member, :main, :] = rounded
        sent_ref[member, main:, :] = halves


def finish_body(neuron_count, own_trials, last, got_ref, gram_ref, raw_ref, *outs):
    neuron_gram_ref, sent_ref, *rest = outs
    size = raw_ref.shape[0]
    total = got_ref[0].astype(jnp.float32)
    for member in range(1, got_ref.shape[0]):
        total = total + got_ref[member].astype(jnp.float32)
    small = total[size : size + PART] + total[size + PART :]
    raw_gram, terms = unpack_small(small, size, own_trials)
    diagonal = raw_gram * eye_of(size)
    down = 1.0 / jnp.sqrt(jnp.sum(diagonal, axis=1, keepdims=True) / neuron_count + tiny_eps)
    across = 1.0 / jnp.sqrt(jnp.sum(diagonal, axis=0, keepdims=True) / neuron_count + tiny_eps)
    neuron_gram = down * raw_gram * across
    neuron_gram_ref[...] = neuron_gram
    trial_own = product(damped_inverse(neuron_gram * gram_ref[...]), terms * down)
    trial_rows = rows_product(eye_of(own_trials), trial_own)
    if last:
        neuron_ref, own_ref = rest
        neuron_ref[...] = raw_ref[...] * down
        own_ref[...] = trial_rows
    else:
        (own_ref,) = rest
        own_ref[...] = trial_own
    columns = [trial_own[:, trial : trial + 1] for trial in range(own_trials)]
    lanes = total.shape[1]
    low = lax.broadcasted_iota(jnp.int32, (size, lanes), 1) < lanes // 2
    same = low == (lax.axis_index("pair") == 0)
    weighted = jnp.where(same, columns[0], columns[1]) * down * total[:size]
    weighted = weighted + pltpu.roll(weighted, lanes // 2, 1)
    half = size // 2
    weighted = jnp.where(low[:half], weighted[:half], weighted[half:])
    tile = tile_of(trial_rows, lanes)
    for member in range(sent_ref.shape[0]):
        sent_ref[member, :half, :] = weighted
        sent_ref[member, half:, :] = tile


def sum_body(own_trials, got_ref, sent_ref, trial_gram_ref):
    _, half, lanes = sent_ref.shape
    total = got_ref[0, :half, :]
    for member in range(1, got_ref.shape[0]):
        total = total + got_ref[member, :half, :]
    for member in range(sent_ref.shape[0]):
        sent_ref[member] = total
    trial_gram_ref[...] = gram_of(trial_of(got_ref, half, own_trials, 2 * half))


def time_of(got_ref, left_ref, right_ref):
    inverse = damped_inverse(left_ref[...] * right_ref[...])
    members, half, lanes = got_ref.shape
    low = lax.broadcasted_iota(jnp.int32, (half, lanes), 1) < lanes // 2
    pieces = []
    for block in range(members // 2):
        one, two = got_ref[block], got_ref[members // 2 + block]
        upper = jnp.where(low, one, pltpu.roll(two, lanes // 2, 1))
        lower = jnp.where(low, pltpu.roll(one, lanes // 2, 1), two)
        pieces.append(jnp.concatenate([upper, lower], axis=0))
    return product(inverse, jnp.concatenate(pieces, axis=1))


def next_body(got_ref, neuron_gram_ref, trial_gram_ref, own_ref, tensor_ref, *outs):
    sent_ref, projected_ref, gram_ref, inverse_ref = outs
    raw = time_of(got_ref, neuron_gram_ref, trial_gram_ref)
    raw_gram = gram_of(raw)
    diagonal = raw_gram * eye_of(raw.shape[0])
    count = raw.shape[1]
    down = 1.0 / jnp.sqrt(jnp.sum(diagonal, axis=1, keepdims=True) / count + tiny_eps)
    across = 1.0 / jnp.sqrt(jnp.sum(diagonal, axis=0, keepdims=True) / count + tiny_eps)
    tensor_of = lambda trial: tensor_ref[trial]
    put_projected(raw * down, own_ref[...], tensor_of, projected_ref, sent_ref)
    gram = down * raw_gram * across
    gram_ref[...] = gram
    inverse_ref[...] = damped_inverse(gram * trial_gram_ref[...])


def last_body(got_ref, neuron_gram_ref, trial_gram_ref, *refs):
    held_neuron_ref, held_own_ref, neuron_ref, time_ref, own_ref = refs
    neuron_ref[...] = held_neuron_ref[...]
    own_ref[...] = held_own_ref[...]
    raw = time_of(got_ref, neuron_gram_ref, trial_gram_ref)
    mean = jnp.sum(raw * raw, axis=1, keepdims=True) / raw.shape[1]
    down = 1.0 / jnp.sqrt(mean + tiny_eps)
    count, size = time_ref.shape
    lanes = got_ref.shape[2]
    position = lax.axis_index(("z", "pair", "y", "core", "x"))
    column = lax.broadcasted_iota(jnp.int32, raw.shape, 1)
    mine = jnp.where(column // count == position, raw, 0.0)
    picked = mine[:, :lanes]
    for start in range(lanes, raw.shape[1], lanes):
        picked = picked + mine[:, start : start + lanes]
    row = lax.broadcasted_iota(jnp.int32, (count, lanes), 0)
    lane = lax.broadcasted_iota(jnp.int32, (count, lanes), 1)
    chosen = (lane == position * count % lanes + row).astype(jnp.float32)
    time_ref[...] = rows_product(chosen, picked * down)


def per_device(tensor, time_init, trial_init):
    own_trials, own_neurons, timepoints = tensor.shape
    components = time_init.shape[0]
    planes = lax.axis_size("x")
    short = ("y", "core")
    near = ("pair",) + short
    blocks, layers = lax.axis_size(short), lax.axis_size("z")
    twins = lax.axis_size("pair")
    neuron_count = own_neurons * blocks * twins * layers
    lanes = timepoints // blocks

    def shape(*dims, kind=jnp.float32):
        return jax.ShapeDtypeStruct(dims, kind)

    square = shape(components, components)
    neuron_outs = (
        shape(components, own_neurons),
        shape(twins * blocks, components + 2 * PART, lanes, kind=WIRE),
    )
    projected_shape = shape(own_trials, components, own_neurons)
    shared, projected, tensor, time_gram = project(
        (
            shape(planes, components + PART, own_neurons),
            projected_shape,
            shape(own_trials, own_neurons, timepoints, kind=tensor.dtype),
            square,
        ),
        time_init,
        trial_init.T,
        tensor,
    )
    shared = lax.all_to_all(shared, "x", 0, 0)
    raw, sent = call(first_neuron_body, neuron_outs, shared, projected, time_gram, tensor)
    for sweep_index in range(SWEEPS):
        got = lax.all_to_all(sent, near, 0, 0)
        sent = call(reduce_body, shape(layers, components + 2 * PART, lanes, kind=WIRE), got)
        got = lax.all_to_all(sent, "z", 0, 0)
        last = sweep_index == SWEEPS - 1
        neuron_shape = shape(components, own_neurons)
        own_shape = shape(own_trials, components)
        extra = (neuron_shape, own_shape) if last else (shape(components, own_trials),)
        neuron_gram, sent, *rest = call(
            lambda *refs: finish_body(neuron_count, own_trials, last, *refs),
            (square, shape(planes, components // 2 + PART, lanes)) + extra,
            got,
            time_gram,
            raw,
        )
        got = lax.all_to_all(sent, "x", 0, 0)
        sent, trial_gram = call(
            lambda *refs: sum_body(own_trials, *refs),
            (shape(twins * blocks, components // 2, lanes), square),
            got,
        )
        got = lax.all_to_all(sent, near, 0, 0)
        if last:
            share_width = timepoints // (layers * twins * blocks * planes)
            neuron_now, time_out, own_trial = call(
                last_body,
                (neuron_shape, shape(share_width, components), own_shape),
                got,
                neuron_gram,
                trial_gram,
                *rest,
                slow=(0, 1, 2),
            )
            break
        shared, projected, time_gram, inverse = call(
            next_body,
            (shape(planes, components, own_neurons), projected_shape, square, square),
            got,
            neuron_gram,
            trial_gram,
            *rest,
            tensor,
        )
        shared = lax.all_to_all(shared, "x", 0, 0)
        raw, sent = call(neuron_body, neuron_outs, shared, projected, inverse, tensor)
    return (neuron_now, time_out.T, own_trial.T)


def solution(mesh):
    neuron, trial = mesh.shape["neuron"], mesh.shape["trial"]
    layers = neuron // 16
    fine = Mesh(
        mesh.devices.reshape(layers, 2, 4, 2, trial), ("z", "pair", "y", "core", "x")
    )
    rows = ("z", "pair", "y", "core")
    return jax.shard_map(
        per_device,
        mesh=fine,
        in_specs=(P("x", rows, None), P(), P(None, "x")),
        out_specs=(P(None, rows), P(None, rows + ("x",)), P(None, "x")),
        check_vma=False,
    )
```

```python
import jax
import jax.numpy as jnp
from jax import lax
from jax.experimental import pallas as pl
from jax.experimental.pallas import tpu as pltpu
from jax.sharding import Mesh, PartitionSpec as P

SWEEPS = 2


ridge_share = 0.1
tiny_eps = 1e-06
EXACT = lax.Precision.HIGHEST
PART = 8
AHEAD = 3
PIECES = 4
WIRE = jnp.bfloat16


def gram_of(matrix):
    return lax.dot_general(
        matrix,
        matrix,
        (((1,), (1,)), ((), ())),
        precision=EXACT,
        preferred_element_type=jnp.float32,
    )


def product(left, right):
    return lax.dot_general(
        left,
        right,
        (((1,), (0,)), ((), ())),
        precision=EXACT,
        preferred_element_type=jnp.float32,
    )


def rows_product(left, right):
    return lax.dot_general(
        left,
        right,
        (((1,), (1,)), ((), ())),
        precision=EXACT,
        preferred_element_type=jnp.float32,
    )


def split(values):
    high = values.astype(WIRE).astype(jnp.float32)
    return jnp.concatenate([high, values - high], axis=0).astype(WIRE)


def eye_of(size):
    rows = lax.broadcasted_iota(jnp.int32, (size, size), 0)
    cols = lax.broadcasted_iota(jnp.int32, (size, size), 1)
    return (rows == cols).astype(jnp.float32)


def damped_inverse(system):
    size = system.shape[0]
    eye = eye_of(size)
    trace = jnp.sum(jnp.sum(system * eye, axis=1, keepdims=True), axis=0, keepdims=True)
    share = size / trace
    both = system * share + ridge_share * eye
    row = lax.broadcasted_iota(jnp.int32, both.shape, 0)
    lane = lax.broadcasted_iota(jnp.int32, both.shape, 1)

    def pivots(step):
        if step >= size:
            return []
        return [
            jnp.broadcast_to(both[:, place : place + 1], both.shape) for place in (step, step + 1)
        ]

    ahead = [pivots(2 * place) for place in range(AHEAD)]
    for step in range(0, size, 2):
        first, second = ahead[0]
        p00, p01 = first[step : step + 1], second[step : step + 1]
        p10, p11 = first[step + 1 : step + 2], second[step + 1 : step + 2]
        over = 1.0 / (p00 * p11 - p01 * p10)
        p00, p01, p10, p11 = p00 * over, p01 * over, p10 * over, p11 * over

        def cleared(matrix):
            upper, lower = matrix[step : step + 1], matrix[step + 1 : step + 2]
            new_upper = p11 * upper - p01 * lower
            new_lower = p00 * lower - p10 * upper
            rest = matrix - first * new_upper - second * new_lower
            return jnp.where(row == step, new_upper, jnp.where(row == step + 1, new_lower, rest))

        ahead = [[cleared(one) for one in pair] for pair in ahead[1:] + [pivots(step + 2 * AHEAD)]]
        inner = jnp.logical_or(lane == step, lane == step + 1)
        both = cleared(jnp.where(inner, eye, both))
    return both * share


def pack_small(gram, terms):
    size = gram.shape[0]
    pieces = []
    for start in range(0, size, PART):
        pieces.append(gram[start : start + PART, start:])
    for start in range(0, size, PART):
        pieces.append(terms[start : start + PART])
    used = sum(piece.shape[1] for piece in pieces)
    pieces.append(jnp.zeros((PART, 128 - used), jnp.float32))
    return jnp.concatenate(pieces, axis=1)


def unpack_small(tile, size, count):
    rows, place = [], 0
    for start in range(0, size, PART):
        piece = tile[:, place : place + size - start]
        place += size - start
        if start:
            piece = jnp.concatenate([jnp.zeros((PART, start), jnp.float32), piece], axis=1)
        rows.append(piece)
    upper = jnp.concatenate(rows, axis=0)
    terms = []
    for start in range(0, size, PART):
        terms.append(tile[:, place : place + count])
        place += count
    row_part = lax.broadcasted_iota(jnp.int32, (size, size), 0) // PART
    col_part = lax.broadcasted_iota(jnp.int32, (size, size), 1) // PART
    return jnp.where(col_part >= row_part, upper, upper.T), jnp.concatenate(terms, axis=0)


def call(body, outs, *args, away=(), slow=()):
    single = not isinstance(outs, tuple)
    listed = (outs,) if single else outs
    args = [
        arg if place in away else pltpu.with_memory_space_constraint(arg, pltpu.VMEM)
        for place, arg in enumerate(args)
    ]
    shapes = tuple(
        out if place in slow else pltpu.VMEM(out.shape, out.dtype)
        for place, out in enumerate(listed)
    )
    result = pl.pallas_call(
        body,
        out_shape=shapes,
        in_specs=[pl.BlockSpec(memory_space=pltpu.VMEM) for _ in args],
        out_specs=tuple(pl.BlockSpec(memory_space=pltpu.VMEM) for _ in listed),
    )(*args)
    return result[0] if single else result


def put_projected(time_now, trial_own, tensor_of, projected_ref, sent_ref):
    rounded = time_now.astype(jnp.bfloat16)
    size = time_now.shape[0]
    part = None
    for trial in range(trial_own.shape[1]):
        projected = lax.dot_general(
            rounded,
            tensor_of(trial),
            (((1,), (1,)), ((), ())),
            preferred_element_type=jnp.float32,
        )
        projected_ref[trial] = projected
        scaled = trial_own[:, trial : trial + 1] * projected
        part = scaled if part is None else part + scaled
    for member in range(sent_ref.shape[0]):
        sent_ref[member, :size, :] = part


def tile_of(rows, lanes):
    count, size = rows.shape
    tile = jnp.concatenate([rows, jnp.zeros((PART - count, size), jnp.float32)], axis=0)
    return jnp.concatenate([tile, jnp.zeros((PART, lanes - size), jnp.float32)], axis=1)


def trial_of(got_ref, start, count, size):
    lines = [got_ref[member, start : start + count, :size] for member in range(got_ref.shape[0])]
    return rows_product(eye_of(size), jnp.concatenate(lines, axis=0))


def project_body(time_hbm, trial_hbm, tensor_hbm, *refs):
    sent_ref, projected_ref, tensor_ref, gram_ref, time_ref, trial_ref, arrived = refs
    count, size = trial_ref.shape
    copies = [
        pltpu.make_async_copy(time_hbm, time_ref, arrived.at[0]),
        pltpu.make_async_copy(trial_hbm, trial_ref, arrived.at[1]),
    ]
    step = tensor_ref.shape[1] // PIECES
    for trial in range(count):
        for piece in range(PIECES):
            rows = pl.ds(piece * step, step)
            copies.append(
                pltpu.make_async_copy(
                    tensor_hbm.at[trial, rows],
                    tensor_ref.at[trial, rows],
                    arrived.at[2 + trial * PIECES + piece],
                )
            )
    for copy in copies:
        copy.start()
    copies[0].wait()
    gram_ref[...] = gram_of(time_ref[...])

    def tensor_of(trial):
        for copy in copies[2 + trial * PIECES : 2 + (trial + 1) * PIECES]:
            copy.wait()
        return tensor_ref[trial]

    copies[1].wait()
    trial_own = rows_product(eye_of(size), trial_ref[...])
    put_projected(time_ref[...], trial_own, tensor_of, projected_ref, sent_ref)
    tile = tile_of(trial_ref[...], sent_ref.shape[2])
    for member in range(sent_ref.shape[0]):
        sent_ref[member, size:, :] = tile


def project(outs, time_init, trial_rows, tensor):
    return pl.pallas_call(
        project_body,
        out_shape=tuple(pltpu.VMEM(out.shape, out.dtype) for out in outs),
        in_specs=[pl.BlockSpec(memory_space=pl.ANY) for _ in range(3)],
        out_specs=tuple(pl.BlockSpec(memory_space=pltpu.VMEM) for _ in outs),
        scratch_shapes=[
            pltpu.VMEM(time_init.shape, time_init.dtype),
            pltpu.VMEM(trial_rows.shape, trial_rows.dtype),
            pltpu.SemaphoreType.DMA((2 + tensor.shape[0] * PIECES,)),
        ],
    )(time_init, trial_rows, tensor)


def put_neuron(inverse, shared_ref, projected_ref, tensor_ref, raw_ref, sent_ref):
    own_trials, size, _ = projected_ref.shape
    neuron_terms = shared_ref[0, :size, :]
    for member in range(1, shared_ref.shape[0]):
        neuron_terms = neuron_terms + shared_ref[member, :size, :]
    raw = product(inverse, neuron_terms)
    raw_ref[...] = raw
    terms = [
        jnp.sum(raw * projected_ref[trial], axis=1, keepdims=True) for trial in range(own_trials)
    ]
    terms = jnp.concatenate(terms, axis=1)
    small = split(pack_small(gram_of(raw), terms))
    members, _, lanes = sent_ref.shape
    blocks = tensor_ref.shape[2] // lanes
    low = lax.broadcasted_iota(jnp.int32, (size, lanes), 1) < lanes // 2
    rounded = raw.astype(jnp.bfloat16)
    first = jnp.dot(rounded, tensor_ref[0], preferred_element_type=jnp.float32)
    second = jnp.dot(rounded, tensor_ref[1], preferred_element_type=jnp.float32)
    for block in range(blocks):
        start = block * lanes
        one = first[:, start : start + lanes]
        two = pltpu.roll(second[:, start : start + lanes], lanes // 2, 1)
        sent_ref[block, :size, :] = jnp.where(low, one, two).astype(WIRE)
        sent_ref[blocks + block, :size, :] = jnp.where(low, two, one).astype(WIRE)
    for member in range(members):
        sent_ref[member, size:, :] = small


def first_neuron_body(shared_ref, projected_ref, gram_ref, tensor_ref, raw_ref, sent_ref):
    own_trials, size, _ = projected_ref.shape
    trial_now = trial_of(shared_ref, size, own_trials, size)
    inverse = damped_inverse(gram_of(trial_now) * gram_ref[...])
    put_neuron(inverse, shared_ref, projected_ref, tensor_ref, raw_ref, sent_ref)


def neuron_body(shared_ref, projected_ref, inverse_ref, tensor_ref, raw_ref, sent_ref):
    put_neuron(inverse_ref[...], shared_ref, projected_ref, tensor_ref, raw_ref, sent_ref)


def reduce_body(got_ref, sent_ref):
    total = got_ref[0].astype(jnp.float32)
    for member in range(1, got_ref.shape[0]):
        total = total + got_ref[member].astype(jnp.float32)
    main = total.shape[0] - 2 * PART
    rounded = total[:main].astype(WIRE)
    halves = split(total[main : main + PART] + total[main + PART :])
    for member in range(sent_ref.shape[0]):
        sent_ref[member, :main, :] = rounded
        sent_ref[member, main:, :] = halves


def finish_body(neuron_count, own_trials, last, got_ref, gram_ref, raw_ref, *outs):
    neuron_gram_ref, sent_ref, *rest = outs
    size = raw_ref.shape[0]
    total = got_ref[0].astype(jnp.float32)
    for member in range(1, got_ref.shape[0]):
        total = total + got_ref[member].astype(jnp.float32)
    small = total[size : size + PART] + total[size + PART :]
    raw_gram, terms = unpack_small(small, size, own_trials)
    diagonal = raw_gram * eye_of(size)
    down = 1.0 / jnp.sqrt(jnp.sum(diagonal, axis=1, keepdims=True) / neuron_count + tiny_eps)
    across = 1.0 / jnp.sqrt(jnp.sum(diagonal, axis=0, keepdims=True) / neuron_count + tiny_eps)
    neuron_gram = down * raw_gram * across
    neuron_gram_ref[...] = neuron_gram
    trial_own = product(damped_inverse(neuron_gram * gram_ref[...]), terms * down)
    trial_rows = rows_product(eye_of(own_trials), trial_own)
    if last:
        neuron_ref, own_ref = rest
        neuron_ref[...] = raw_ref[...] * down
        own_ref[...] = trial_rows
    else:
        (own_ref,) = rest
        own_ref[...] = trial_own
    columns = [trial_own[:, trial : trial + 1] for trial in range(own_trials)]
    lanes = total.shape[1]
    low = lax.broadcasted_iota(jnp.int32, (size, lanes), 1) < lanes // 2
    same = low == (lax.axis_index("pair") == 0)
    weighted = jnp.where(same, columns[0], columns[1]) * down * total[:size]
    weighted = weighted + pltpu.roll(weighted, lanes // 2, 1)
    half = size // 2
    weighted = jnp.where(low[:half], weighted[:half], weighted[half:])
    tile = tile_of(trial_rows, lanes)
    for member in range(sent_ref.shape[0]):
        sent_ref[member, :half, :] = weighted
        sent_ref[member, half:, :] = tile


def sum_body(own_trials, got_ref, sent_ref, trial_rows_ref):
    _, half, lanes = sent_ref.shape
    total = got_ref[0, :half, :]
    for member in range(1, got_ref.shape[0]):
        total = total + got_ref[member, :half, :]
    for member in range(sent_ref.shape[0]):
        sent_ref[member] = total
    for member in range(got_ref.shape[0]):
        trial_rows_ref[member * own_trials : (member + 1) * own_trials, :] = got_ref[
            member, half : half + own_trials, : 2 * half
        ]


def time_of(got_ref, neuron_gram_ref, trial_gram):
    inverse = damped_inverse(neuron_gram_ref[...] * trial_gram)
    members, half, lanes = got_ref.shape
    low = lax.broadcasted_iota(jnp.int32, (half, lanes), 1) < lanes // 2
    pieces = []
    for block in range(members // 2):
        one, two = got_ref[block], got_ref[members // 2 + block]
        upper = jnp.where(low, one, pltpu.roll(two, lanes // 2, 1))
        lower = jnp.where(low, pltpu.roll(one, lanes // 2, 1), two)
        pieces.append(jnp.concatenate([upper, lower], axis=0))
    return product(inverse, jnp.concatenate(pieces, axis=1))


def next_body(got_ref, neuron_gram_ref, trial_rows_ref, own_ref, tensor_ref, *outs):
    sent_ref, projected_ref, gram_ref, inverse_ref = outs
    trial_gram = gram_of(rows_product(eye_of(trial_rows_ref.shape[1]), trial_rows_ref[...]))
    raw = time_of(got_ref, neuron_gram_ref, trial_gram)
    raw_gram = gram_of(raw)
    diagonal = raw_gram * eye_of(raw.shape[0])
    count = raw.shape[1]
    down = 1.0 / jnp.sqrt(jnp.sum(diagonal, axis=1, keepdims=True) / count + tiny_eps)
    across = 1.0 / jnp.sqrt(jnp.sum(diagonal, axis=0, keepdims=True) / count + tiny_eps)
    tensor_of = lambda trial: tensor_ref[trial]
    put_projected(raw * down, own_ref[...], tensor_of, projected_ref, sent_ref)
    gram = down * raw_gram * across
    gram_ref[...] = gram
    inverse_ref[...] = damped_inverse(gram * trial_gram)


def last_body(got_ref, neuron_gram_ref, trial_rows_ref, *refs):
    held_neuron_ref, held_own_ref, neuron_ref, time_ref, own_ref = refs
    neuron_ref[...] = held_neuron_ref[...]
    own_ref[...] = held_own_ref[...]
    trial_gram = gram_of(rows_product(eye_of(trial_rows_ref.shape[1]), trial_rows_ref[...]))
    raw = time_of(got_ref, neuron_gram_ref, trial_gram)
    mean = jnp.sum(raw * raw, axis=1, keepdims=True) / raw.shape[1]
    down = 1.0 / jnp.sqrt(mean + tiny_eps)
    count, size = time_ref.shape
    lanes = got_ref.shape[2]
    position = lax.axis_index(("z", "pair", "y", "core", "x"))
    column = lax.broadcasted_iota(jnp.int32, raw.shape, 1)
    mine = jnp.where(column // count == position, raw, 0.0)
    picked = mine[:, :lanes]
    for start in range(lanes, raw.shape[1], lanes):
        picked = picked + mine[:, start : start + lanes]
    row = lax.broadcasted_iota(jnp.int32, (count, lanes), 0)
    lane = lax.broadcasted_iota(jnp.int32, (count, lanes), 1)
    chosen = (lane == position * count % lanes + row).astype(jnp.float32)
    time_ref[...] = rows_product(chosen, picked * down)


def per_device(tensor, time_init, trial_init):
    own_trials, own_neurons, timepoints = tensor.shape
    components = time_init.shape[0]
    planes = lax.axis_size("x")
    short = ("y", "core")
    near = ("pair",) + short
    blocks, layers = lax.axis_size(short), lax.axis_size("z")
    twins = lax.axis_size("pair")
    neuron_count = own_neurons * blocks * twins * layers
    lanes = timepoints // blocks

    def shape(*dims, kind=jnp.float32):
        return jax.ShapeDtypeStruct(dims, kind)

    square = shape(components, components)
    neuron_outs = (
        shape(components, own_neurons),
        shape(twins * blocks, components + 2 * PART, lanes, kind=WIRE),
    )
    projected_shape = shape(own_trials, components, own_neurons)
    shared, projected, tensor, time_gram = project(
        (
            shape(planes, components + PART, own_neurons),
            projected_shape,
            shape(own_trials, own_neurons, timepoints, kind=tensor.dtype),
            square,
        ),
        time_init,
        trial_init.T,
        tensor,
    )
    shared = lax.all_to_all(shared, "x", 0, 0)
    raw, sent = call(first_neuron_body, neuron_outs, shared, projected, time_gram, tensor)
    for sweep_index in range(SWEEPS):
        got = lax.all_to_all(sent, near, 0, 0)
        sent = call(reduce_body, shape(layers, components + 2 * PART, lanes, kind=WIRE), got)
        got = lax.all_to_all(sent, "z", 0, 0)
        last = sweep_index == SWEEPS - 1
        neuron_shape = shape(components, own_neurons)
        own_shape = shape(own_trials, components)
        extra = (neuron_shape, own_shape) if last else (shape(components, own_trials),)
        neuron_gram, sent, *rest = call(
            lambda *refs: finish_body(neuron_count, own_trials, last, *refs),
            (square, shape(planes, components // 2 + PART, lanes)) + extra,
            got,
            time_gram,
            raw,
        )
        got = lax.all_to_all(sent, "x", 0, 0)
        sent, trial_rows = call(
            lambda *refs: sum_body(own_trials, *refs),
            (
                shape(twins * blocks, components // 2, lanes),
                shape(planes * own_trials, components),
            ),
            got,
        )
        got = lax.all_to_all(sent, near, 0, 0)
        if last:
            share_width = timepoints // (layers * twins * blocks * planes)
            neuron_now, time_out, own_trial = call(
                last_body,
                (neuron_shape, shape(share_width, components), own_shape),
                got,
                neuron_gram,
                trial_rows,
                *rest,
                slow=(0, 1, 2),
            )
            break
        shared, projected, time_gram, inverse = call(
            next_body,
            (shape(planes, components, own_neurons), projected_shape, square, square),
            got,
            neuron_gram,
            trial_rows,
            *rest,
            tensor,
        )
        shared = lax.all_to_all(shared, "x", 0, 0)
        raw, sent = call(neuron_body, neuron_outs, shared, projected, inverse, tensor)
    return (neuron_now, time_out.T, own_trial.T)


def solution(mesh):
    neuron, trial = mesh.shape["neuron"], mesh.shape["trial"]
    layers = neuron // 16
    fine = Mesh(
        mesh.devices.reshape(layers, 2, 4, 2, trial), ("z", "pair", "y", "core", "x")
    )
    rows = ("z", "pair", "y", "core")
    return jax.shard_map(
        per_device,
        mesh=fine,
        in_specs=(P("x", rows, None), P(), P(None, "x")),
        out_specs=(P(None, rows), P(None, rows + ("x",)), P(None, "x")),
        check_vma=False,
    )
```
